256 devices in a mesh: row: 16 (over z, core), col: 16 (over y, x).
Axes of the slice: x: 4, y: 4, z: 8, core: 2. Of those that a mesh axis runs over, the one named last changes fastest.
Arguments:
- inputs: bfloat16 [2048, 8192], P('col', 'row'), may hold values from -6 to 6
- weight: bfloat16 [8192, 28672], P('row', 'col'), may hold values from -0.09375 to 0.09375
- mask: int32 [64, 224], P('row', 'col'), may hold values 0 or 1
- cotangent: bfloat16 [2048, 28672], P('row', 'col'), may hold values from -6 to 6
Outputs:
- outputs: bfloat16 [2048, 28672], P('row', 'col')
- input_grad: bfloat16 [2048, 8192], P('col', 'row')
- weight_grad: bfloat16 [8192, 28672], P('row', 'col')
The draws below stay inside these ranges and needn't reach their ends.
Inputs may be any that keep to these rules, and one draw needn't show every extreme that they name: mask holds only zeros and ones.
All inputs are finite; a program needn't handle non-finite values. No bound on the sum of `mask` on one device may be relied on, other than what follows from the above.
Results may differ from the reference program's by a relative error of at most 0.022.
Values may be sent and summed in bfloat16 or wider, within the bound.
A program may use at most 128 MiB of HBM per device.

```python
import jax
import jax.numpy as jnp
from jax import lax

D = 8192
F = 28672
BLOCK = 128
TOKENS = 2048
N_ROW = 16
N_COL = 16


def plant(entries, own_key, smallest, largest):
    dims = entries.shape
    index_at = [jax.random.randint(jax.random.fold_in(own_key, axis), (), 0, dims[axis]) for axis in range(len(dims))]
    entries = entries.at[tuple(index_at)].set(smallest)
    longest = dims.index(max(dims))
    index_at[longest] = (index_at[longest] + 1) % dims[longest]
    return entries.at[tuple(index_at)].set(largest)


def spiked(result, stream_key, source, target, shards_of, factor):
    def block_of(dim):
        return (jnp.arange(result.shape[dim]) // (result.shape[dim] // shards_of)).reshape((-1,) + (1,) * (result.ndim - 1 - dim))

    near = jax.random.permutation(stream_key, shards_of)[block_of(target)]
    far = (block_of(target) + shards_of // 2) % shards_of
    return jnp.where((block_of(source) == near) | (block_of(source) == far), factor * result, result)


def level_of(stream_key, dims, shards, smallest, high):
    level = 1.0
    for position, blocks in shards:
        heights = jax.random.uniform(jax.random.fold_in(jax.random.fold_in(stream_key, 6), position), (blocks,), jnp.float32, smallest / len(shards), high / len(shards))
        level = level * jnp.repeat(jnp.exp(heights), dims[position] // blocks).reshape((-1,) + (1,) * (len(dims) - 1 - position))
    return level


def bell_draw(key, dims, deviation, bound, pieces=(), kind=jnp.bfloat16):
    level = level_of(key, dims, pieces, -0.22, 0.18) if pieces else 1.0
    array = jax.random.normal(key, dims, jnp.float32) * deviation * level
    return jnp.minimum(jnp.maximum(array, -bound), bound).astype(kind)


def bell_draw_with(stream_key, extent, spread, reach, cuts, heavy, held_as=jnp.bfloat16):
    result = spread * jax.random.normal(stream_key, extent, jnp.float32)
    if cuts:
        result = result * level_of(stream_key, extent, cuts, -0.22, 0.18)
    return jnp.clip(spiked(result, jax.random.fold_in(stream_key, 3), *heavy), -reach, reach).astype(held_as)


def setup_inputs(seed: int = 0) -> dict:
    splits = jax.random.split(jax.random.key(seed), 5)
    return {
        "inputs": bell_draw_with(splits[0], (TOKENS, D), 1.0, 6.0, ((0, 16), (1, 16)), (1, 0, 16, 2.0)),
        "weight": bell_draw(splits[1], (D, F), (D // 2) ** -0.5, 0.09375, ((0, 16), (1, 16))),
        "mask": plant((jax.random.randint(splits[2], (D // BLOCK, F // BLOCK), 0, 2) < 1).astype(jnp.int32), jax.random.fold_in(splits[2], 1), 0, 1),
        "cotangent": bell_draw_with(splits[3], (TOKENS, F), 1.0, 6.0, ((0, 16), (1, 16)), (1, 0, 16, 2.0)),
    }


def expand_mask(mask_tile):
    tile_rows, tile_cols = mask_tile.shape
    mask_float = mask_tile.astype(jnp.float32)
    widened = jnp.broadcast_to(mask_float[:, None, :, None], (tile_rows, BLOCK, tile_cols, BLOCK))
    return widened.reshape(tile_rows * BLOCK, tile_cols * BLOCK)


def rounded(value):
    return lax.optimization_barrier(value.astype(jnp.bfloat16)).astype(jnp.float32)


def reference(inputs, weight, mask, cotangent):
    keep_mask = expand_mask(mask)
    masked = (weight.astype(jnp.float32) * keep_mask).astype(jnp.bfloat16)
    row_width = D // N_ROW
    col_width = F // N_COL
    forward_acc = jnp.zeros((TOKENS, F), jnp.float32)
    for row_index in range(N_ROW):
        lower_edge = row_index * row_width
        upper_edge = lower_edge + row_width
        partial_value = jnp.dot(inputs[:, lower_edge:upper_edge], masked[lower_edge:upper_edge, :], preferred_element_type=jnp.float32)
        forward_acc = forward_acc + rounded(partial_value)
    outputs = forward_acc.astype(jnp.bfloat16)
    grad_acc = jnp.zeros((TOKENS, D), jnp.float32)
    for col_index in range(N_COL):
        lower_edge = col_index * col_width
        upper_edge = lower_edge + col_width
        partial_value = lax.dot_general(cotangent[:, lower_edge:upper_edge], masked[:, lower_edge:upper_edge], (((1,), (1,)), ((), ())), preferred_element_type=jnp.float32)
        grad_acc = grad_acc + rounded(partial_value)
    input_grad = grad_acc.astype(jnp.bfloat16)
    product = lax.dot_general(inputs, cotangent, (((0,), (0,)), ((), ())), preferred_element_type=jnp.float32)
    weight_grad = (product * keep_mask * (TOKENS ** -0.5)).astype(jnp.bfloat16)
    return outputs, input_grad, weight_grad
```

```python
import functools

import jax
import jax.numpy as jnp
from jax import lax
from jax.experimental import pallas as pl
from jax.experimental.pallas import tpu as pltpu
from jax.sharding import PartitionSpec as P

BLOCK = 128
NZ = 8
NC = 16
F32 = jnp.float32
BF16 = jnp.bfloat16
UP, DOWN = 0, 1


def remote(src, dst, send_sem, recv_sem, device):
    return pltpu.make_async_remote_copy(
        src_ref=src,
        dst_ref=dst,
        send_sem=send_sem,
        recv_sem=recv_sem,
        device_id=device,
        device_id_type=pl.DeviceIdType.MESH,
    )


def kernel(
    scale,
    x_hbm, w_hbm, mask_smem, c_hbm,
    out_hbm, ig_hbm, wg_hbm,
    X, XT, W, WT, C, PO, PS_out, PS, S, R, G, GR, WG, OUT, IG,
    load_sem, x_send, x_recv, az_send, az_recv, as_send, as_recv,
    ps_send, ps_recv, r_send, r_recv, g_send, g_recv, store_sem,
):
    row = lax.axis_index("row")
    col = lax.axis_index("col")
    z, core = row // 2, row % 2
    tok, width = c_hbm.shape
    depth = x_hbm.shape[1]
    half = tok // 2
    up = ((row + 2) % (2 * NZ), col)
    down = ((row + 2 * NZ - 2) % (2 * NZ), col)
    sibling = (row + 1 - 2 * core, col)
    toward = (up, down)
    my_rows = core * tok

    def partner(j):
        xx, yy = col % 4, col // 4
        return ((yy + j // 4) % 4) * 4 + (xx + j % 4) % 4

    def sender(j):
        xx, yy = col % 4, col // 4
        return ((yy + 4 - j // 4) % 4) * 4 + (xx + 4 - j % 4) % 4

    load_c = pltpu.make_async_copy(c_hbm, C.at[pl.ds(my_rows, tok)], load_sem.at[0])
    load_x = pltpu.make_async_copy(x_hbm, X.at[col], load_sem.at[1])
    load_w = pltpu.make_async_copy(w_hbm, W, load_sem.at[2])
    load_c.start()
    load_x.start()
    load_w.start()

    barrier = pltpu.get_barrier_semaphore()
    for device in (up, down, sibling):
        pl.semaphore_signal(barrier, inc=1, device_id=device, device_id_type=pl.DeviceIdType.MESH)

    def greet(j, carry):
        pl.semaphore_signal(barrier, inc=1, device_id=(row, partner(j)), device_id_type=pl.DeviceIdType.MESH)
        return carry

    lax.fori_loop(1, NC, greet, 0)
    pl.semaphore_wait(barrier, NC + 2)

    def chunk(rel, part, owner=core):
        return C.at[pl.ds(rel * 2 * tok + owner * tok + part * half, half)]

    def gather_copy(way, part, dist):
        rel = (-dist if way == UP else dist) % NZ
        land = (rel - 1 if way == UP else rel + 1) % NZ
        return remote(chunk(rel, part), chunk(land, part), az_send.at[way, part, dist], az_recv.at[way, part, dist], toward[way])

    def share_copy(rel, part):
        return remote(chunk(rel, part), chunk(rel, part), as_send.at[rel, part], as_recv.at[rel, part], sibling)

    def share_wait(rel):
        for part in range(2):
            other = chunk(rel, part, 1 - core)
            remote(other, other, as_send.at[rel, part], as_recv.at[rel, part], sibling).wait_recv()

    def last(way, part):
        return NZ // 2 if part == way else NZ // 2 - 1

    load_c.wait()
    for part in range(2):
        for way in (UP, DOWN):
            gather_copy(way, part, 0).start()
    for part in range(2):
        share_copy(0, part).start()
    load_x.wait()

    def x_copy(j):
        return remote(X.at[col], X.at[col], x_send.at[j], x_recv.at[j], (row, partner(j)))

    def x_start(j, carry):
        x_copy(j).start()
        return carry

    lax.fori_loop(1, NC, x_start, 0)

    def x_wait(j, carry):
        land = X.at[sender(j)]
        remote(land, land, x_send.at[j], x_recv.at[j], (row, partner(j))).wait_recv()
        return carry

    load_w.wait()
    rows_w, cols_w = depth // BLOCK, width // BLOCK

    def mask_rows(i, carry):
        at = pl.ds(pl.multiple_of(i * BLOCK, BLOCK), BLOCK)
        for j in range(cols_w):
            to = pl.ds(j * BLOCK, BLOCK)
            keep = mask_smem[i, j].astype(F32)
            W[at, to] = (W[at, to].astype(F32) * keep).astype(BF16)
        return carry

    lax.fori_loop(0, rows_w, mask_rows, 0)

    def flip(j, carry):
        at = pl.ds(pl.multiple_of(j * 256, 256), 256)
        WT[at, :] = W[:, at].T
        return carry

    lax.fori_loop(0, width // 256, flip, 0)

    def gather_step(dist):
        for part in range(2):
            for way in (UP, DOWN):
                if dist > last(way, part):
                    continue
                gather_copy(way, part, dist - 1).wait_recv()
                if dist < last(way, part):
                    gather_copy(way, part, dist).start()
                rel = (-dist if way == UP else dist) % NZ
                share_copy(rel, part).start()

    def grad_partial(rel):
        share_wait(rel)
        value = jnp.dot(C[pl.ds(rel * 2 * tok, 2 * tok), :], WT[...], preferred_element_type=F32).astype(BF16)
        there = 2 * ((z + rel) % NZ)
        for owner in range(2):
            dest = there + owner
            G[rel, owner] = value[owner * tok:(owner + 1) * tok]

            @pl.when(dest == col)
            def _():
                GR[dest] = G[rel, owner]

            @pl.when(dest != col)
            def _():
                remote(G.at[rel, owner], GR.at[col], g_send.at[rel, owner], g_recv.at[col], (row, dest)).start()

    def product(rel, carry):
        there = (z + rel) % NZ
        x_pair = X[pl.ds(2 * there, 2)].reshape(2 * tok, depth)
        XT[:, pl.ds(pl.multiple_of(rel * 2 * tok, 2 * tok), 2 * tok)] = x_pair.T

        def column(n, carry):
            at = pl.ds(pl.multiple_of(n * 256, 256), 256)
            value = jnp.dot(x_pair, W[:, at], preferred_element_type=F32)
            first, second = value[:tok], value[tok:]
            PO[rel, :, at] = jnp.where(core == 0, first, second)
            PS_out[rel, :, at] = jnp.where(core == 0, second, first).astype(BF16)
            return carry

        lax.fori_loop(0, width // 256, column, 0)
        pair_copy(rel).start()
        return carry

    def pair_copy(rel):
        return remote(PS_out.at[rel], PS.at[rel], ps_send.at[rel], ps_recv.at[rel], sibling)

    def reduce_copy(way, part, dist):
        return remote(S.at[way, part, dist], R.at[way, part, dist], r_send.at[way, part, dist], r_recv.at[way, part, dist], toward[way])

    def reduce_send(way, part, dist):
        rel = (dist if way == UP else -dist) % NZ
        at = pl.ds(part * half, half)
        total = PO[rel, at, :] + PS[rel, at, :].astype(F32)
        if dist < last(way, part):
            reduce_copy(way, part, dist + 1).wait_recv()
            total += R[way, part, dist + 1].astype(F32)
        S[way, part, dist] = total.astype(BF16)
        reduce_copy(way, part, dist).start()

    def reduce_step(step):
        for way in (UP, DOWN):
            for part in (way, 1 - way):
                dist = last(way, part) - step
                if dist >= 1:
                    reduce_send(way, part, dist)

    gather_step(1)
    grad_partial(0)
    gather_step(2)
    grad_partial(1)
    grad_partial(NZ - 1)
    gather_step(3)
    lax.fori_loop(1, NC, x_wait, 0)
    lax.fori_loop(0, NZ, product, 0)
    gather_step(4)
    for rel in range(NZ):
        pair_copy(rel).wait_recv()
    reduce_step(0)
    for rel in (2, 3, 4, 5, 6):
        grad_partial(rel)
    reduce_step(1)

    def weight_grad(n, carry):
        at = pl.ds(pl.multiple_of(n * 256, 256), 256)
        value = jnp.dot(XT[...], C[:, at], preferred_element_type=F32)
        for i in range(rows_w):
            for j in range(2):
                keep = mask_smem[i, n * 2 + j].astype(F32) * scale
                piece = value[i * BLOCK:(i + 1) * BLOCK, j * BLOCK:(j + 1) * BLOCK] * keep
                WG[pl.ds(i * BLOCK, BLOCK), pl.ds(pl.multiple_of(n * 256 + j * BLOCK, BLOCK), BLOCK)] = piece.astype(BF16)
        return carry

    lax.fori_loop(0, width // 256, weight_grad, 0)
    store_wg = pltpu.make_async_copy(WG, wg_hbm, store_sem.at[0])
    store_wg.start()
    reduce_step(2)

    def g_wait(j, carry):
        other = (col + j) % NC
        remote(GR.at[other], GR.at[other], g_send.at[0, 0], g_recv.at[other], (row, other)).wait_recv()
        return carry

    lax.fori_loop(1, NC, g_wait, 0)

    def g_sum(i, carry):
        at = pl.ds(pl.multiple_of(i * 16, 16), 16)
        total = GR[0, at, :].astype(F32)
        for c in range(1, NC):
            total += GR[c, at, :].astype(F32)
        IG[at, :] = total.astype(BF16)
        return carry

    lax.fori_loop(0, tok // 16, g_sum, 0)
    store_ig = pltpu.make_async_copy(IG, ig_hbm, store_sem.at[1])
    store_ig.start()
    reduce_step(3)

    for part in range(2):
        for way in (UP, DOWN):
            reduce_copy(way, part, 1).wait_recv()
        at = pl.ds(part * half, half)
        total = PO[0, at, :] + PS[0, at, :].astype(F32)
        total += R[UP, part, 1].astype(F32) + R[DOWN, part, 1].astype(F32)
        OUT[at, :] = total.astype(BF16)
    store_out = pltpu.make_async_copy(OUT, out_hbm, store_sem.at[2])
    store_out.start()

    for part in range(2):
        for way in (UP, DOWN):
            for dist in range(last(way, part)):
                gather_copy(way, part, dist).wait_send()
                reduce_copy(way, part, dist + 1).wait_send()
        for rel in range(NZ):
            share_copy(rel, part).wait_send()
    for rel in range(NZ):
        pair_copy(rel).wait_send()
        for owner in range(2):
            dest = 2 * ((z + rel) % NZ) + owner

            @pl.when(dest != col)
            def _():
                remote(G.at[rel, owner], GR.at[col], g_send.at[rel, owner], g_recv.at[col], (row, dest)).wait_send()

    def x_sent(j, carry):
        x_copy(j).wait_send()
        return carry

    lax.fori_loop(1, NC, x_sent, 0)
    store_wg.wait()
    store_ig.wait()
    store_out.wait()


def local(inputs, weight, mask, cotangent):
    tok, depth = inputs.shape
    width = weight.shape[1]
    half = tok // 2
    steps = NZ // 2 + 1
    dma = pltpu.SemaphoreType.DMA
    hbm = pl.BlockSpec(memory_space=pl.ANY)
    tokens = tok * NC
    return pl.pallas_call(
        functools.partial(kernel, float(tokens) ** -0.5),
        out_shape=(
            jax.ShapeDtypeStruct((tok, width), BF16),
            jax.ShapeDtypeStruct((tok, depth), BF16),
            jax.ShapeDtypeStruct((depth, width), BF16),
        ),
        in_specs=[hbm, hbm, pl.BlockSpec(memory_space=pltpu.SMEM), hbm],
        out_specs=(hbm, hbm, hbm),
        scratch_shapes=[
            pltpu.VMEM((NC, tok, depth), BF16),
            pltpu.VMEM((depth, tokens), BF16),
            pltpu.VMEM((depth, width), BF16),
            pltpu.VMEM((width, depth), BF16),
            pltpu.VMEM((tokens, width), BF16),
            pltpu.VMEM((NZ, tok, width), F32),
            pltpu.VMEM((NZ, tok, width), BF16),
            pltpu.VMEM((NZ, tok, width), BF16),
            pltpu.VMEM((2, 2, steps, half, width), BF16),
            pltpu.VMEM((2, 2, steps, half, width), BF16),
            pltpu.VMEM((NZ, 2, tok, depth), BF16),
            pltpu.VMEM((NC, tok, depth), BF16),
            pltpu.VMEM((depth, width), BF16),
            pltpu.VMEM((tok, width), BF16),
            pltpu.VMEM((tok, depth), BF16),
            dma((3,)),
            dma((NC,)), dma((NC,)),
            dma((2, 2, steps)), dma((2, 2, steps)),
            dma((NZ, 2)), dma((NZ, 2)),
            dma((NZ,)), dma((NZ,)),
            dma((2, 2, steps)), dma((2, 2, steps)),
            dma((NZ, 2)), dma((NC,)),
            dma((3,)),
        ],
        compiler_params=pltpu.CompilerParams(
            collective_id=0, has_side_effects=True, vmem_limit_bytes=60 * 1024 * 1024
        ),
        cost_estimate=pl.CostEstimate(
            flops=6 * tokens * depth * width, bytes_accessed=4 * depth * width + 4 * tok * (width + depth), transcendentals=0
        ),
    )(inputs, weight, mask, cotangent)


def solution(mesh):
    placed = (P("col", "row"), P("row", "col"), P("row", "col"), P("row", "col"))
    return jax.shard_map(
        local,
        mesh=mesh,
        in_specs=placed,
        out_specs=(P("row", "col"), P("col", "row"), P("row", "col")),
        check_vma=False,
    )
```

```python
import functools

import jax
import jax.numpy as jnp
from jax import lax
from jax.experimental import pallas as pl
from jax.experimental.pallas import tpu as pltpu
from jax.sharding import PartitionSpec as P

BLOCK = 128
NZ = 8
NC = 16
F32 = jnp.float32
BF16 = jnp.bfloat16
UP, DOWN = 0, 1


def remote(src, dst, send_sem, recv_sem, device):
    return pltpu.make_async_remote_copy(
        src_ref=src,
        dst_ref=dst,
        send_sem=send_sem,
        recv_sem=recv_sem,
        device_id=device,
        device_id_type=pl.DeviceIdType.MESH,
    )


def kernel(
    scale,
    x_hbm, w_hbm, mask_smem, c_hbm,
    out_hbm, ig_hbm, wg_hbm,
    X, XT, W, WT, C, PO, PS_out, PS, S, R, G, GR, WG, OUT, IG,
    load_sem, x_send, x_recv, az_send, az_recv, as_send, as_recv,
    ps_send, ps_recv, r_send, r_recv, g_send, g_recv, store_sem,
):
    row = lax.axis_index("row")
    col = lax.axis_index("col")
    z, core = row // 2, row % 2
    tok, width = c_hbm.shape
    depth = x_hbm.shape[1]
    half = tok // 2
    up = ((row + 2) % (2 * NZ), col)
    down = ((row + 2 * NZ - 2) % (2 * NZ), col)
    sibling = (row + 1 - 2 * core, col)
    toward = (up, down)
    my_rows = core * tok

    cx, cy = col % 4, col // 4

    def step_x(n):
        return (row, cy * 4 + (cx + n + 4) % 4)

    def step_y(n):
        return (row, ((cy + n + 4) % 4) * 4 + cx)

    load_c = pltpu.make_async_copy(c_hbm, C.at[pl.ds(my_rows, tok)], load_sem.at[0])
    load_x = pltpu.make_async_copy(x_hbm, X.at[cy, cx], load_sem.at[1])
    load_w = pltpu.make_async_copy(w_hbm, W, load_sem.at[2])
    load_c.start()
    load_x.start()
    load_w.start()

    barrier = pltpu.get_barrier_semaphore()
    for device in (up, down, sibling):
        pl.semaphore_signal(barrier, inc=1, device_id=device, device_id_type=pl.DeviceIdType.MESH)

    def greet(j, carry):
        pl.semaphore_signal(barrier, inc=1, device_id=(row, (col + j) % NC), device_id_type=pl.DeviceIdType.MESH)
        return carry

    lax.fori_loop(1, NC, greet, 0)
    pl.semaphore_wait(barrier, NC + 2)

    def chunk(rel, part, owner=core):
        return C.at[pl.ds(rel * 2 * tok + owner * tok + part * half, half)]

    def gather_copy(way, part, dist):
        rel = (-dist if way == UP else dist) % NZ
        land = (rel - 1 if way == UP else rel + 1) % NZ
        return remote(chunk(rel, part), chunk(land, part), az_send.at[way, part, dist], az_recv.at[way, part, dist], toward[way])

    def share_copy(rel, part):
        return remote(chunk(rel, part), chunk(rel, part), as_send.at[rel, part], as_recv.at[rel, part], sibling)

    def share_wait(rel):
        for part in range(2):
            other = chunk(rel, part, 1 - core)
            remote(other, other, as_send.at[rel, part], as_recv.at[rel, part], sibling).wait_recv()

    def last(way, part):
        return NZ // 2 if part == way else NZ // 2 - 1

    quarter = half // 2

    def x_copy(h, stage, way):
        sign = 1 if way == UP else -1
        step = (step_x if (h == 0) == (stage < 2) else step_y)(sign)
        back = 0 if stage % 2 == 0 else -sign
        rows = pl.ds(h * half, half) if stage % 2 == 0 else pl.ds(h * half + way * quarter, quarter)
        if stage < 2:
            xs, ys = ((cx + back + 4) % 4, cy) if h == 0 else (cx, (cy + back + 4) % 4)
            block = X.at[ys, xs, rows]
        elif h == 0:
            block = X.at[(cy + back + 4) % 4, :, rows]
        else:
            block = X.at[:, (cx + back + 4) % 4, rows]
        return remote(block, block, x_send.at[h, stage, way], x_recv.at[h, stage, way], step)

    def x_stage(stage):
        for h in range(2):
            for way in (UP, DOWN):
                if stage % 2 == 1:
                    x_copy(h, stage - 1, way).wait_recv()
                    x_copy(h, stage, way).start()
            if stage % 2 == 0:
                for way in (UP, DOWN):
                    if stage:
                        x_copy(h, stage - 1, way).wait_recv()
                for way in (UP, DOWN):
                    if stage < 4:
                        x_copy(h, stage, way).start()

    load_c.wait()
    for way in (UP, DOWN):
        gather_copy(way, 0, 0).start()
    load_x.wait()
    x_stage(0)
    for way in (UP, DOWN):
        gather_copy(way, 1, 0).start()
    for part in range(2):
        share_copy(0, part).start()

    load_w.wait()
    rows_w, cols_w = depth // BLOCK, width // BLOCK

    def mask_rows(i, carry):
        at = pl.ds(pl.multiple_of(i * BLOCK, BLOCK), BLOCK)
        for j in range(cols_w):
            to = pl.ds(j * BLOCK, BLOCK)
            keep = mask_smem[i, j].astype(F32)
            W[at, to] = (W[at, to].astype(F32) * keep).astype(BF16)
        return carry

    lax.fori_loop(0, rows_w, mask_rows, 0)

    def flip(j, carry):
        at = pl.ds(pl.multiple_of(j * 256, 256), 256)
        WT[at, :] = W[:, at].T
        return carry

    lax.fori_loop(0, width // 256, flip, 0)

    def gather_step(dist, lead):
        for way in (UP, DOWN):
            part = way if lead else 1 - way
            gather_copy(way, part, dist - 1).wait_recv()
            if dist < last(way, part):
                gather_copy(way, part, dist).start()
            rel = (-dist if way == UP else dist) % NZ
            share_copy(rel, part).start()

    def grad_partial(rel):
        share_wait(rel)
        value = jnp.dot(C[pl.ds(rel * 2 * tok, 2 * tok), :], WT[...], preferred_element_type=F32).astype(BF16)
        there = 2 * ((z + rel) % NZ)
        for owner in range(2):
            dest = there + owner
            G[rel, owner] = value[owner * tok:(owner + 1) * tok]

            @pl.when(dest == col)
            def _():
                GR[dest] = G[rel, owner]

            @pl.when(dest != col)
            def _():
                remote(G.at[rel, owner], GR.at[col], g_send.at[rel, owner], g_recv.at[col], (row, dest)).start()

    def product(rel):
        there = (z + rel) % NZ
        x_pair = X[there // 2, pl.ds(2 * (there % 2), 2)].reshape(2 * tok, depth)
        XT[:, pl.ds(rel * 2 * tok, 2 * tok)] = x_pair.T

        def column(n, carry):
            at = pl.ds(pl.multiple_of(n * 256, 256), 256)
            value = jnp.dot(x_pair, W[:, at], preferred_element_type=F32)
            first, second = value[:tok], value[tok:]
            PO[rel, :, at] = jnp.where(core == 0, first, second)
            PS_out[rel, :, at] = jnp.where(core == 0, second, first).astype(BF16)
            return carry

        lax.fori_loop(0, width // 256, column, 0)
        pair_copy(rel).start()

    def pair_copy(rel):
        return remote(PS_out.at[rel], PS.at[rel], ps_send.at[rel], ps_recv.at[rel], sibling)

    def reduce_copy(way, part, dist):
        return remote(S.at[way, part, dist], R.at[way, part, dist], r_send.at[way, part, dist], r_recv.at[way, part, dist], toward[way])

    def reduce_send(way, part, dist):
        rel = (dist if way == UP else -dist) % NZ
        at = pl.ds(part * half, half)
        total = PO[rel, at, :] + PS[rel, at, :].astype(F32)
        if dist < last(way, part):
            reduce_copy(way, part, dist + 1).wait_recv()
            total += R[way, part, dist + 1].astype(F32)
        S[way, part, dist] = total.astype(BF16)
        reduce_copy(way, part, dist).start()

    def reduce_step(step, lead):
        for way in (UP, DOWN):
            part = way if lead else 1 - way
            reduce_send(way, part, last(way, part) - step)

    def weight_grad(n, carry):
        at = pl.ds(pl.multiple_of(n * 256, 256), 256)
        value = jnp.dot(XT[...], C[:, at], preferred_element_type=F32)
        for i in range(rows_w):
            for j in range(2):
                keep = mask_smem[i, n * 2 + j].astype(F32) * scale
                piece = value[i * BLOCK:(i + 1) * BLOCK, j * BLOCK:(j + 1) * BLOCK] * keep
                WG[pl.ds(i * BLOCK, BLOCK), pl.ds(pl.multiple_of(n * 256 + j * BLOCK, BLOCK), BLOCK)] = piece.astype(BF16)
        return carry

    x_stage(1)
    grad_partial(0)
    x_stage(2)
    gather_step(1, True)
    gather_step(1, False)
    x_stage(3)
    grad_partial(1)
    grad_partial(7)
    gather_step(2, True)
    x_stage(4)
    for rel in (4, 3, 5):
        product(rel)
    gather_step(2, False)
    for rel in (2, 6):
        product(rel)
    grad_partial(2)
    grad_partial(6)
    gather_step(3, True)
    for rel in (1, 7, 0):
        product(rel)
    for rel in (4, 3, 5):
        pair_copy(rel).wait_recv()
    reduce_step(0, True)
    reduce_step(0, False)
    gather_step(3, False)
    grad_partial(3)
    grad_partial(5)
    gather_step(4, True)
    grad_partial(4)
    for rel in (2, 6, 1, 7, 0):
        pair_copy(rel).wait_recv()
    reduce_step(1, True)
    lax.fori_loop(0, 2, weight_grad, 0)
    reduce_step(1, False)
    lax.fori_loop(2, 4, weight_grad, 0)
    reduce_step(2, True)
    lax.fori_loop(4, 6, weight_grad, 0)
    reduce_step(2, False)
    lax.fori_loop(6, width // 256, weight_grad, 0)
    store_wg = pltpu.make_async_copy(WG, wg_hbm, store_sem.at[0])
    store_wg.start()
    reduce_step(3, True)

    def g_wait(j, carry):
        other = (col + j) % NC
        remote(GR.at[other], GR.at[other], g_send.at[0, 0], g_recv.at[other], (row, other)).wait_recv()
        return carry

    lax.fori_loop(1, NC, g_wait, 0)

    def g_sum(i, carry):
        at = pl.ds(pl.multiple_of(i * 16, 16), 16)
        total = GR[0, at, :].astype(F32)
        for c in range(1, NC):
            total += GR[c, at, :].astype(F32)
        IG[at, :] = total.astype(BF16)
        return carry

    lax.fori_loop(0, tok // 16, g_sum, 0)
    store_ig = pltpu.make_async_copy(IG, ig_hbm, store_sem.at[1])
    store_ig.start()

    for part in range(2):
        for way in (UP, DOWN):
            reduce_copy(way, part, 1).wait_recv()
        at = pl.ds(part * half, half)
        total = PO[0, at, :] + PS[0, at, :].astype(F32)
        total += R[UP, part, 1].astype(F32) + R[DOWN, part, 1].astype(F32)
        OUT[at, :] = total.astype(BF16)
    store_out = pltpu.make_async_copy(OUT, out_hbm, store_sem.at[2])
    store_out.start()

    for part in range(2):
        for way in (UP, DOWN):
            for dist in range(last(way, part)):
                gather_copy(way, part, dist).wait_send()
                reduce_copy(way, part, dist + 1).wait_send()
        for rel in range(NZ):
            share_copy(rel, part).wait_send()
    for rel in range(NZ):
        pair_copy(rel).wait_send()
        for owner in range(2):
            dest = 2 * ((z + rel) % NZ) + owner

            @pl.when(dest != col)
            def _():
                remote(G.at[rel, owner], GR.at[col], g_send.at[rel, owner], g_recv.at[col], (row, dest)).wait_send()

    for h in range(2):
        for stage in range(4):
            for way in (UP, DOWN):
                x_copy(h, stage, way).wait_send()
    store_wg.wait()
    store_ig.wait()
    store_out.wait()


def finish(out_in, ig_in, wg_in, out_hbm, ig_hbm, wg_hbm, OUT, IG, WG, sem):
    rows = WG.shape[0] // 4
    moves = [(wg_in.at[pl.ds(i * rows, rows)], WG.at[pl.ds(i * rows, rows)], wg_hbm.at[pl.ds(i * rows, rows)]) for i in range(4)]
    moves += [(out_in, OUT, out_hbm), (ig_in, IG, ig_hbm)]
    loads = [pltpu.make_async_copy(a, b, sem.at[0, i]) for i, (a, b, _) in enumerate(moves)]
    stores = [pltpu.make_async_copy(b, c, sem.at[1, i]) for i, (_, b, c) in enumerate(moves)]
    for load in loads:
        load.start()
    for load, store in zip(loads, stores):
        load.wait()
        store.start()
    for store in stores:
        store.wait()


def local(inputs, weight, mask, cotangent):
    tok, depth = inputs.shape
    width = weight.shape[1]
    half = tok // 2
    steps = NZ // 2 + 1
    dma = pltpu.SemaphoreType.DMA
    hbm = pl.BlockSpec(memory_space=pl.ANY)
    tokens = tok * NC
    results = pl.pallas_call(
        functools.partial(kernel, float(tokens) ** -0.5),
        out_shape=(
            jax.ShapeDtypeStruct((tok, width), BF16),
            jax.ShapeDtypeStruct((tok, depth), BF16),
            jax.ShapeDtypeStruct((depth, width), BF16),
        ),
        in_specs=[hbm, hbm, pl.BlockSpec(memory_space=pltpu.SMEM), hbm],
        out_specs=(hbm, hbm, hbm),
        scratch_shapes=[
            pltpu.VMEM((4, 4, tok, depth), BF16),
            pltpu.VMEM((depth, tokens), BF16),
            pltpu.VMEM((depth, width), BF16),
            pltpu.VMEM((width, depth), BF16),
            pltpu.VMEM((tokens, width), BF16),
            pltpu.VMEM((NZ, tok, width), F32),
            pltpu.VMEM((NZ, tok, width), BF16),
            pltpu.VMEM((NZ, tok, width), BF16),
            pltpu.VMEM((2, 2, steps, half, width), BF16),
            pltpu.VMEM((2, 2, steps, half, width), BF16),
            pltpu.VMEM((NZ, 2, tok, depth), BF16),
            pltpu.VMEM((NC, tok, depth), BF16),
            pltpu.VMEM((depth, width), BF16),
            pltpu.VMEM((tok, width), BF16),
            pltpu.VMEM((tok, depth), BF16),
            dma((3,)),
            dma((2, 4, 2)), dma((2, 4, 2)),
            dma((2, 2, steps)), dma((2, 2, steps)),
            dma((NZ, 2)), dma((NZ, 2)),
            dma((NZ,)), dma((NZ,)),
            dma((2, 2, steps)), dma((2, 2, steps)),
            dma((NZ, 2)), dma((NC,)),
            dma((3,)),
        ],
        compiler_params=pltpu.CompilerParams(
            collective_id=0, has_side_effects=True, vmem_limit_bytes=60 * 1024 * 1024
        ),
        cost_estimate=pl.CostEstimate(
            flops=6 * tokens * depth * width, bytes_accessed=4 * depth * width + 4 * tok * (width + depth), transcendentals=0
        ),
    )(inputs, weight, mask, cotangent)
    return pl.pallas_call(
        finish,
        out_shape=tuple(jax.ShapeDtypeStruct(r.shape, r.dtype) for r in results),
        in_specs=[hbm] * 3,
        out_specs=(hbm,) * 3,
        scratch_shapes=[pltpu.VMEM(r.shape, r.dtype) for r in results] + [dma((2, 6))],
        compiler_params=pltpu.CompilerParams(vmem_limit_bytes=60 * 1024 * 1024),
    )(*results)


def solution(mesh):
    placed = (P("col", "row"), P("row", "col"), P("row", "col"), P("row", "col"))
    return jax.shard_map(
        local,
        mesh=mesh,
        in_specs=placed,
        out_specs=(P("row", "col"), P("col", "row"), P("row", "col")),
        check_vma=False,
    )
```

```python
import functools

import jax
import jax.numpy as jnp
from jax import lax
from jax.experimental import pallas as pl
from jax.experimental.pallas import tpu as pltpu
from jax.sharding import PartitionSpec as P

BLOCK = 128
NZ = 8
NC = 16
F32 = jnp.float32
BF16 = jnp.bfloat16
UP, DOWN = 0, 1


def remote(src, dst, send_sem, recv_sem, device):
    return pltpu.make_async_remote_copy(
        src_ref=src,
        dst_ref=dst,
        send_sem=send_sem,
        recv_sem=recv_sem,
        device_id=device,
        device_id_type=pl.DeviceIdType.MESH,
    )


def kernel(
    scale,
    x_hbm, w_hbm, mask_smem, c_hbm,
    out_hbm, ig_hbm, wg_hbm,
    X, XT, W, WT, C, PO, PS_out, PS, S, R, G, GR, WG, OUT, IG,
    load_sem, x_send, x_recv, az_send, az_recv, as_send, as_recv,
    ps_send, ps_recv, r_send, r_recv, g_send, g_recv, store_sem,
):
    row = lax.axis_index("row")
    col = lax.axis_index("col")
    z, core = row // 2, row % 2
    tok, width = c_hbm.shape
    depth = x_hbm.shape[1]
    half = tok // 2
    up = ((row + 2) % (2 * NZ), col)
    down = ((row + 2 * NZ - 2) % (2 * NZ), col)
    sibling = (row + 1 - 2 * core, col)
    toward = (up, down)
    my_rows = core * tok

    cx, cy = col % 4, col // 4

    def step_x(n):
        return (row, cy * 4 + (cx + n + 4) % 4)

    def step_y(n):
        return (row, ((cy + n + 4) % 4) * 4 + cx)

    load_c = pltpu.make_async_copy(c_hbm, C.at[pl.ds(my_rows, tok)], load_sem.at[0])
    load_x = pltpu.make_async_copy(x_hbm, X.at[cy, cx], load_sem.at[1])
    load_w = pltpu.make_async_copy(w_hbm, W, load_sem.at[2])
    load_c.start()
    load_x.start()
    load_w.start()

    barrier = pltpu.get_barrier_semaphore()
    for device in (up, down, sibling):
        pl.semaphore_signal(barrier, inc=1, device_id=device, device_id_type=pl.DeviceIdType.MESH)

    def greet(j, carry):
        pl.semaphore_signal(barrier, inc=1, device_id=(row, (col + j) % NC), device_id_type=pl.DeviceIdType.MESH)
        return carry

    lax.fori_loop(1, NC, greet, 0)
    pl.semaphore_wait(barrier, NC + 2)

    def chunk(rel, part, owner=core):
        return C.at[pl.ds(rel * 2 * tok + owner * tok + part * half, half)]

    def gather_copy(way, part, dist):
        rel = (-dist if way == UP else dist) % NZ
        land = (rel - 1 if way == UP else rel + 1) % NZ
        return remote(chunk(rel, part), chunk(land, part), az_send.at[way, part, dist], az_recv.at[way, part, dist], toward[way])

    def share_copy(rel, part):
        return remote(chunk(rel, part), chunk(rel, part), as_send.at[rel, part], as_recv.at[rel, part], sibling)

    def share_wait(rel):
        for part in range(2):
            other = chunk(rel, part, 1 - core)
            remote(other, other, as_send.at[rel, part], as_recv.at[rel, part], sibling).wait_recv()

    def last(way, part):
        return NZ // 2 if part == way else NZ // 2 - 1

    quarter = half // 2

    def x_copy(h, stage, way):
        sign = 1 if way == UP else -1
        step = (step_x if (h == 0) == (stage < 2) else step_y)(sign)
        back = 0 if stage % 2 == 0 else -sign
        rows = pl.ds(h * half, half) if stage % 2 == 0 else pl.ds(h * half + way * quarter, quarter)
        if stage < 2:
            xs, ys = ((cx + back + 4) % 4, cy) if h == 0 else (cx, (cy + back + 4) % 4)
            block = X.at[ys, xs, rows]
        elif h == 0:
            block = X.at[(cy + back + 4) % 4, :, rows]
        else:
            block = X.at[:, (cx + back + 4) % 4, rows]
        return remote(block, block, x_send.at[h, stage, way], x_recv.at[h, stage, way], step)

    def x_stage(stage):
        for h in range(2):
            for way in (UP, DOWN):
                if stage % 2 == 1:
                    x_copy(h, stage - 1, way).wait_recv()
                    x_copy(h, stage, way).start()
            if stage % 2 == 0:
                for way in (UP, DOWN):
                    if stage:
                        x_copy(h, stage - 1, way).wait_recv()
                for way in (UP, DOWN):
                    if stage < 4:
                        x_copy(h, stage, way).start()

    load_c.wait()
    for way in (UP, DOWN):
        gather_copy(way, 0, 0).start()
    load_x.wait()
    x_stage(0)
    for way in (UP, DOWN):
        gather_copy(way, 1, 0).start()
    for part in range(2):
        share_copy(0, part).start()

    load_w.wait()
    rows_w, cols_w = depth // BLOCK, width // BLOCK

    def mask_rows(i, carry):
        at = pl.ds(pl.multiple_of(i * BLOCK, BLOCK), BLOCK)
        for j in range(cols_w):
            to = pl.ds(j * BLOCK, BLOCK)
            keep = mask_smem[i, j].astype(F32)
            W[at, to] = (W[at, to].astype(F32) * keep).astype(BF16)
        return carry

    lax.fori_loop(0, rows_w, mask_rows, 0)

    def flip(j, carry):
        at = pl.ds(pl.multiple_of(j * 256, 256), 256)
        WT[at, :] = W[:, at].T
        return carry

    lax.fori_loop(0, width // 256, flip, 0)

    def gather_step(dist, lead):
        for way in (UP, DOWN):
            part = way if lead else 1 - way
            gather_copy(way, part, dist - 1).wait_recv()
            if dist < last(way, part):
                gather_copy(way, part, dist).start()
            rel = (-dist if way == UP else dist) % NZ
            share_copy(rel, part).start()

    def grad_partial(rel):
        share_wait(rel)
        value = jnp.dot(C[pl.ds(rel * 2 * tok, 2 * tok), :], WT[...], preferred_element_type=F32).astype(BF16)
        there = 2 * ((z + rel) % NZ)
        for owner in range(2):
            dest = there + owner
            G[rel, owner] = value[owner * tok:(owner + 1) * tok]

            @pl.when(dest == col)
            def _():
                GR[dest] = G[rel, owner]

            @pl.when(dest != col)
            def _():
                remote(G.at[rel, owner], GR.at[col], g_send.at[rel, owner], g_recv.at[col], (row, dest)).start()

    def product(rel):
        there = (z + rel) % NZ
        x_pair = X[there // 2, pl.ds(2 * (there % 2), 2)].reshape(2 * tok, depth)
        XT[:, pl.ds(rel * 2 * tok, 2 * tok)] = x_pair.T

        def column(n, carry):
            at = pl.ds(pl.multiple_of(n * 256, 256), 256)
            value = jnp.dot(x_pair, W[:, at], preferred_element_type=F32)
            first, second = value[:tok], value[tok:]
            PO[rel, :, at] = jnp.where(core == 0, first, second)
            PS_out[rel, :, at] = jnp.where(core == 0, second, first).astype(BF16)
            return carry

        lax.fori_loop(0, width // 256, column, 0)
        pair_copy(rel).start()

    def pair_copy(rel):
        return remote(PS_out.at[rel], PS.at[rel], ps_send.at[rel], ps_recv.at[rel], sibling)

    def reduce_copy(way, part, dist):
        return remote(S.at[way, part, dist], R.at[way, part, dist], r_send.at[way, part, dist], r_recv.at[way, part, dist], toward[way])

    def reduce_send(way, part, dist):
        rel = (dist if way == UP else -dist) % NZ
        at = pl.ds(part * half, half)
        total = PO[rel, at, :] + PS[rel, at, :].astype(F32)
        if dist < last(way, part):
            reduce_copy(way, part, dist + 1).wait_recv()
            total += R[way, part, dist + 1].astype(F32)
        S[way, part, dist] = total.astype(BF16)
        reduce_copy(way, part, dist).start()

    def reduce_step(step, lead):
        for way in (UP, DOWN):
            part = way if lead else 1 - way
            reduce_send(way, part, last(way, part) - step)

    def weight_grad(n, carry):
        at = pl.ds(pl.multiple_of(n * 256, 256), 256)
        value = jnp.dot(XT[...], C[:, at], preferred_element_type=F32)
        for i in range(rows_w):
            for j in range(2):
                keep = mask_smem[i, n * 2 + j].astype(F32) * scale
                piece = value[i * BLOCK:(i + 1) * BLOCK, j * BLOCK:(j + 1) * BLOCK] * keep
                WG[pl.ds(i * BLOCK, BLOCK), pl.ds(pl.multiple_of(n * 256 + j * BLOCK, BLOCK), BLOCK)] = piece.astype(BF16)
        return carry

    x_stage(1)
    x_stage(2)
    gather_step(1, True)
    gather_step(1, False)
    x_stage(3)
    gather_step(2, True)
    x_stage(4)
    for rel in (4, 3, 5):
        product(rel)
    grad_partial(0)
    gather_step(2, False)
    for rel in (2, 6):
        product(rel)
    grad_partial(1)
    grad_partial(7)
    gather_step(3, True)
    for rel in (1, 7, 0):
        product(rel)
    for rel in (4, 3, 5):
        pair_copy(rel).wait_recv()
    reduce_step(0, True)
    reduce_step(0, False)
    grad_partial(2)
    grad_partial(6)
    gather_step(3, False)
    grad_partial(3)
    grad_partial(5)
    gather_step(4, True)
    grad_partial(4)
    for rel in (2, 6, 1, 7, 0):
        pair_copy(rel).wait_recv()
    reduce_step(1, True)
    lax.fori_loop(0, 2, weight_grad, 0)
    reduce_step(1, False)
    lax.fori_loop(2, 4, weight_grad, 0)
    reduce_step(2, True)
    lax.fori_loop(4, 6, weight_grad, 0)
    reduce_step(2, False)
    lax.fori_loop(6, width // 256, weight_grad, 0)
    store_wg = pltpu.make_async_copy(WG, wg_hbm, store_sem.at[0])
    store_wg.start()
    reduce_step(3, True)

    def g_wait(j, carry):
        other = (col + j) % NC
        remote(GR.at[other], GR.at[other], g_send.at[0, 0], g_recv.at[other], (row, other)).wait_recv()
        return carry

    lax.fori_loop(1, NC, g_wait, 0)

    def g_sum(i, carry):
        at = pl.ds(pl.multiple_of(i * 16, 16), 16)
        total = GR[0, at, :].astype(F32)
        for c in range(1, NC):
            total += GR[c, at, :].astype(F32)
        IG[at, :] = total.astype(BF16)
        return carry

    lax.fori_loop(0, tok // 16, g_sum, 0)
    store_ig = pltpu.make_async_copy(IG, ig_hbm, store_sem.at[1])
    store_ig.start()

    for part in range(2):
        for way in (UP, DOWN):
            reduce_copy(way, part, 1).wait_recv()
        at = pl.ds(part * half, half)
        total = PO[0, at, :] + PS[0, at, :].astype(F32)
        total += R[UP, part, 1].astype(F32) + R[DOWN, part, 1].astype(F32)
        OUT[at, :] = total.astype(BF16)
    store_out = pltpu.make_async_copy(OUT, out_hbm, store_sem.at[2])
    store_out.start()

    for part in range(2):
        for way in (UP, DOWN):
            for dist in range(last(way, part)):
                gather_copy(way, part, dist).wait_send()
                reduce_copy(way, part, dist + 1).wait_send()
        for rel in range(NZ):
            share_copy(rel, part).wait_send()
    for rel in range(NZ):
        pair_copy(rel).wait_send()
        for owner in range(2):
            dest = 2 * ((z + rel) % NZ) + owner

            @pl.when(dest != col)
            def _():
                remote(G.at[rel, owner], GR.at[col], g_send.at[rel, owner], g_recv.at[col], (row, dest)).wait_send()

    for h in range(2):
        for stage in range(4):
            for way in (UP, DOWN):
                x_copy(h, stage, way).wait_send()
    store_wg.wait()
    store_ig.wait()
    store_out.wait()


def finish(out_in, ig_in, wg_in, out_hbm, ig_hbm, wg_hbm, OUT, IG, WG, sem):
    rows = WG.shape[0] // 4
    moves = [(wg_in.at[pl.ds(i * rows, rows)], WG.at[pl.ds(i * rows, rows)], wg_hbm.at[pl.ds(i * rows, rows)]) for i in range(4)]
    moves += [(out_in, OUT, out_hbm), (ig_in, IG, ig_hbm)]
    loads = [pltpu.make_async_copy(a, b, sem.at[0, i]) for i, (a, b, _) in enumerate(moves)]
    stores = [pltpu.make_async_copy(b, c, sem.at[1, i]) for i, (_, b, c) in enumerate(moves)]
    for load in loads:
        load.start()
    for load, store in zip(loads, stores):
        load.wait()
        store.start()
    for store in stores:
        store.wait()


def local(inputs, weight, mask, cotangent):
    tok, depth = inputs.shape
    width = weight.shape[1]
    half = tok // 2
    steps = NZ // 2 + 1
    dma = pltpu.SemaphoreType.DMA
    hbm = pl.BlockSpec(memory_space=pl.ANY)
    tokens = tok * NC
    results = pl.pallas_call(
        functools.partial(kernel, float(tokens) ** -0.5),
        out_shape=(
            jax.ShapeDtypeStruct((tok, width), BF16),
            jax.ShapeDtypeStruct((tok, depth), BF16),
            jax.ShapeDtypeStruct((depth, width), BF16),
        ),
        in_specs=[hbm, hbm, pl.BlockSpec(memory_space=pltpu.SMEM), hbm],
        out_specs=(hbm, hbm, hbm),
        scratch_shapes=[
            pltpu.VMEM((4, 4, tok, depth), BF16),
            pltpu.VMEM((depth, tokens), BF16),
            pltpu.VMEM((depth, width), BF16),
            pltpu.VMEM((width, depth), BF16),
            pltpu.VMEM((tokens, width), BF16),
            pltpu.VMEM((NZ, tok, width), F32),
            pltpu.VMEM((NZ, tok, width), BF16),
            pltpu.VMEM((NZ, tok, width), BF16),
            pltpu.VMEM((2, 2, steps, half, width), BF16),
            pltpu.VMEM((2, 2, steps, half, width), BF16),
            pltpu.VMEM((NZ, 2, tok, depth), BF16),
            pltpu.VMEM((NC, tok, depth), BF16),
            pltpu.VMEM((depth, width), BF16),
            pltpu.VMEM((tok, width), BF16),
            pltpu.VMEM((tok, depth), BF16),
            dma((3,)),
            dma((2, 4, 2)), dma((2, 4, 2)),
            dma((2, 2, steps)), dma((2, 2, steps)),
            dma((NZ, 2)), dma((NZ, 2)),
            dma((NZ,)), dma((NZ,)),
            dma((2, 2, steps)), dma((2, 2, steps)),
            dma((NZ, 2)), dma((NC,)),
            dma((3,)),
        ],
        compiler_params=pltpu.CompilerParams(
            collective_id=0, has_side_effects=True, vmem_limit_bytes=60 * 1024 * 1024
        ),
        cost_estimate=pl.CostEstimate(
            flops=6 * tokens * depth * width, bytes_accessed=4 * depth * width + 4 * tok * (width + depth), transcendentals=0
        ),
    )(inputs, weight, mask, cotangent)
    return pl.pallas_call(
        finish,
        out_shape=tuple(jax.ShapeDtypeStruct(r.shape, r.dtype) for r in results),
        in_specs=[hbm] * 3,
        out_specs=(hbm,) * 3,
        scratch_shapes=[pltpu.VMEM(r.shape, r.dtype) for r in results] + [dma((2, 6))],
        compiler_params=pltpu.CompilerParams(vmem_limit_bytes=60 * 1024 * 1024),
    )(*results)


def solution(mesh):
    placed = (P("col", "row"), P("row", "col"), P("row", "col"), P("row", "col"))
    return jax.shard_map(
        local,
        mesh=mesh,
        in_specs=placed,
        out_specs=(P("row", "col"), P("col", "row"), P("row", "col")),
        check_vma=False,
    )
```

```python
import functools

import jax
import jax.numpy as jnp
from jax import lax
from jax.experimental import pallas as pl
from jax.experimental.pallas import tpu as pltpu
from jax.sharding import PartitionSpec as P

BLOCK = 128
NZ = 8
NC = 16
F32 = jnp.float32
BF16 = jnp.bfloat16
UP, DOWN = 0, 1


def remote(src, dst, send_sem, recv_sem, device):
    return pltpu.make_async_remote_copy(
        src_ref=src,
        dst_ref=dst,
        send_sem=send_sem,
        recv_sem=recv_sem,
        device_id=device,
        device_id_type=pl.DeviceIdType.MESH,
    )


def kernel(
    scale,
    x_hbm, w_hbm, mask_smem, c_hbm,
    out_hbm, ig_hbm, wg_hbm,
    X, XT, W, WT, C, PO, PS_out, PS, S, R, G, GR, WG, OUT, IG,
    load_sem, x_send, x_recv, az_send, az_recv, as_send, as_recv,
    ps_send, ps_recv, r_send, r_recv, g_send, g_recv, store_sem,
):
    row = lax.axis_index("row")
    col = lax.axis_index("col")
    z, core = row // 2, row % 2
    tok, width = c_hbm.shape
    depth = x_hbm.shape[1]
    half = tok // 2
    up = ((row + 2) % (2 * NZ), col)
    down = ((row + 2 * NZ - 2) % (2 * NZ), col)
    sibling = (row + 1 - 2 * core, col)
    toward = (up, down)
    my_rows = core * tok

    cx, cy = col % 4, col // 4

    def step_x(n):
        return (row, cy * 4 + (cx + n + 4) % 4)

    def step_y(n):
        return (row, ((cy + n + 4) % 4) * 4 + cx)

    load_c = pltpu.make_async_copy(c_hbm, C.at[pl.ds(my_rows, tok)], load_sem.at[0])
    load_x = pltpu.make_async_copy(x_hbm, X.at[cy, cx], load_sem.at[1])
    load_w = pltpu.make_async_copy(w_hbm, W, load_sem.at[2])
    load_c.start()
    load_x.start()
    load_w.start()

    barrier = pltpu.get_barrier_semaphore()
    neighbours = (up, down, sibling, step_x(1), step_x(-1), step_y(1), step_y(-1))
    for device in neighbours:
        pl.semaphore_signal(barrier, inc=1, device_id=device, device_id_type=pl.DeviceIdType.MESH)
    pl.semaphore_wait(barrier, len(neighbours))

    def chunk(rel, part, owner=core):
        return C.at[pl.ds(rel * 2 * tok + owner * tok + part * half, half)]

    def gather_copy(way, part, dist):
        rel = (-dist if way == UP else dist) % NZ
        land = (rel - 1 if way == UP else rel + 1) % NZ
        return remote(chunk(rel, part), chunk(land, part), az_send.at[way, part, dist], az_recv.at[way, part, dist], toward[way])

    def share_copy(rel, part):
        return remote(chunk(rel, part), chunk(rel, part), as_send.at[rel, part], as_recv.at[rel, part], sibling)

    def share_wait(rel):
        for part in range(2):
            other = chunk(rel, part, 1 - core)
            remote(other, other, as_send.at[rel, part], as_recv.at[rel, part], sibling).wait_recv()

    def last(way, part):
        return NZ // 2 if part == way else NZ // 2 - 1

    quarter = half // 2

    def x_copy(h, stage, way):
        sign = 1 if way == UP else -1
        step = (step_x if (h == 0) == (stage < 2) else step_y)(sign)
        back = 0 if stage % 2 == 0 else -sign
        rows = pl.ds(h * half, half) if stage % 2 == 0 else pl.ds(h * half + way * quarter, quarter)
        if stage < 2:
            xs, ys = ((cx + back + 4) % 4, cy) if h == 0 else (cx, (cy + back + 4) % 4)
            block = X.at[ys, xs, rows]
        elif h == 0:
            block = X.at[(cy + back + 4) % 4, :, rows]
        else:
            block = X.at[:, (cx + back + 4) % 4, rows]
        return remote(block, block, x_send.at[h, stage, way], x_recv.at[h, stage, way], step)

    def x_stage(stage):
        for h in range(2):
            for way in (UP, DOWN):
                if stage % 2 == 1:
                    x_copy(h, stage - 1, way).wait_recv()
                    x_copy(h, stage, way).start()
            if stage % 2 == 0:
                for way in (UP, DOWN):
                    if stage:
                        x_copy(h, stage - 1, way).wait_recv()
                for way in (UP, DOWN):
                    if stage < 4:
                        x_copy(h, stage, way).start()

    load_c.wait()
    for way in (UP, DOWN):
        gather_copy(way, 0, 0).start()
    load_x.wait()
    x_stage(0)
    for way in (UP, DOWN):
        gather_copy(way, 1, 0).start()
    for part in range(2):
        share_copy(0, part).start()

    load_w.wait()
    rows_w, cols_w = depth // BLOCK, width // BLOCK

    def mask_rows(i, carry):
        at = pl.ds(pl.multiple_of(i * BLOCK, BLOCK), BLOCK)
        for j in range(cols_w):
            to = pl.ds(j * BLOCK, BLOCK)
            keep = mask_smem[i, j].astype(F32)
            W[at, to] = (W[at, to].astype(F32) * keep).astype(BF16)
        return carry

    lax.fori_loop(0, rows_w, mask_rows, 0)

    def flip(j, carry):
        at = pl.ds(pl.multiple_of(j * 256, 256), 256)
        WT[at, :] = W[:, at].T
        return carry

    lax.fori_loop(0, width // 256, flip, 0)

    def gather_step(dist, lead):
        for way in (UP, DOWN):
            part = way if lead else 1 - way
            gather_copy(way, part, dist - 1).wait_recv()
            if dist < last(way, part):
                gather_copy(way, part, dist).start()
            rel = (-dist if way == UP else dist) % NZ
            share_copy(rel, part).start()

    def grad_partial(rel):
        share_wait(rel)
        value = jnp.dot(C[pl.ds(rel * 2 * tok, 2 * tok), :], WT[...], preferred_element_type=F32).astype(BF16)
        there = 2 * ((z + rel) % NZ)
        for owner in range(2):
            dest = there + owner
            G[rel, owner] = value[owner * tok:(owner + 1) * tok]

            @pl.when(dest == col)
            def _():
                GR[dest] = G[rel, owner]

            @pl.when(dest != col)
            def _():
                remote(G.at[rel, owner], GR.at[col], g_send.at[rel, owner], g_recv.at[col], (row, dest)).start()

    def product(rel):
        there = (z + rel) % NZ
        x_pair = X[there // 2, pl.ds(2 * (there % 2), 2)].reshape(2 * tok, depth)
        XT[:, pl.ds(rel * 2 * tok, 2 * tok)] = x_pair.T

        def column(n, carry):
            at = pl.ds(pl.multiple_of(n * 256, 256), 256)
            value = jnp.dot(x_pair, W[:, at], preferred_element_type=F32)
            first, second = value[:tok], value[tok:]
            PO[rel, :, at] = jnp.where(core == 0, first, second)
            PS_out[rel, :, at] = jnp.where(core == 0, second, first).astype(BF16)
            return carry

        lax.fori_loop(0, width // 256, column, 0)
        pair_copy(rel).start()

    def pair_copy(rel):
        return remote(PS_out.at[rel], PS.at[rel], ps_send.at[rel], ps_recv.at[rel], sibling)

    def reduce_copy(way, part, dist):
        return remote(S.at[way, part, dist], R.at[way, part, dist], r_send.at[way, part, dist], r_recv.at[way, part, dist], toward[way])

    def reduce_send(way, part, dist):
        rel = (dist if way == UP else -dist) % NZ
        at = pl.ds(part * half, half)
        total = PO[rel, at, :] + PS[rel, at, :].astype(F32)
        if dist < last(way, part):
            reduce_copy(way, part, dist + 1).wait_recv()
            total += R[way, part, dist + 1].astype(F32)
        S[way, part, dist] = total.astype(BF16)
        reduce_copy(way, part, dist).start()

    def reduce_step(step, lead):
        for way in (UP, DOWN):
            part = way if lead else 1 - way
            reduce_send(way, part, last(way, part) - step)

    def weight_grad(n, carry):
        at = pl.ds(pl.multiple_of(n * 256, 256), 256)
        value = jnp.dot(XT[...], C[:, at], preferred_element_type=F32)
        for i in range(rows_w):
            for j in range(2):
                keep = mask_smem[i, n * 2 + j].astype(F32) * scale
                piece = value[i * BLOCK:(i + 1) * BLOCK, j * BLOCK:(j + 1) * BLOCK] * keep
                WG[pl.ds(i * BLOCK, BLOCK), pl.ds(pl.multiple_of(n * 256 + j * BLOCK, BLOCK), BLOCK)] = piece.astype(BF16)
        return carry

    x_stage(1)
    x_stage(2)
    gather_step(1, True)
    gather_step(1, False)
    x_stage(3)
    gather_step(2, True)
    x_stage(4)
    for rel in (4, 3, 5):
        product(rel)
    grad_partial(0)
    gather_step(2, False)
    for rel in (2, 6):
        product(rel)
    grad_partial(1)
    grad_partial(7)
    gather_step(3, True)
    for rel in (1, 7, 0):
        product(rel)
    for rel in (4, 3, 5):
        pair_copy(rel).wait_recv()
    reduce_step(0, True)
    reduce_step(0, False)
    grad_partial(2)
    grad_partial(6)
    gather_step(3, False)
    grad_partial(3)
    grad_partial(5)
    gather_step(4, True)
    grad_partial(4)
    for rel in (2, 6, 1, 7, 0):
        pair_copy(rel).wait_recv()
    reduce_step(1, True)
    lax.fori_loop(0, 2, weight_grad, 0)
    reduce_step(1, False)
    lax.fori_loop(2, 4, weight_grad, 0)
    reduce_step(2, True)
    lax.fori_loop(4, 6, weight_grad, 0)
    reduce_step(2, False)
    lax.fori_loop(6, width // 256, weight_grad, 0)
    store_wg = pltpu.make_async_copy(WG, wg_hbm, store_sem.at[0])
    store_wg.start()
    reduce_step(3, True)

    def g_wait(j, carry):
        other = (col + j) % NC
        remote(GR.at[other], GR.at[other], g_send.at[0, 0], g_recv.at[other], (row, other)).wait_recv()
        return carry

    lax.fori_loop(1, NC, g_wait, 0)

    def g_sum(i, carry):
        at = pl.ds(pl.multiple_of(i * 16, 16), 16)
        total = GR[0, at, :].astype(F32)
        for c in range(1, NC):
            total += GR[c, at, :].astype(F32)
        IG[at, :] = total.astype(BF16)
        return carry

    lax.fori_loop(0, tok // 16, g_sum, 0)
    store_ig = pltpu.make_async_copy(IG, ig_hbm, store_sem.at[1])
    store_ig.start()

    for part in range(2):
        for way in (UP, DOWN):
            reduce_copy(way, part, 1).wait_recv()
        at = pl.ds(part * half, half)
        total = PO[0, at, :] + PS[0, at, :].astype(F32)
        total += R[UP, part, 1].astype(F32) + R[DOWN, part, 1].astype(F32)
        OUT[at, :] = total.astype(BF16)
    store_out = pltpu.make_async_copy(OUT, out_hbm, store_sem.at[2])
    store_out.start()

    for part in range(2):
        for way in (UP, DOWN):
            for dist in range(last(way, part)):
                gather_copy(way, part, dist).wait_send()
                reduce_copy(way, part, dist + 1).wait_send()
        for rel in range(NZ):
            share_copy(rel, part).wait_send()
    for rel in range(NZ):
        pair_copy(rel).wait_send()
        for owner in range(2):
            dest = 2 * ((z + rel) % NZ) + owner

            @pl.when(dest != col)
            def _():
                remote(G.at[rel, owner], GR.at[col], g_send.at[rel, owner], g_recv.at[col], (row, dest)).wait_send()

    for h in range(2):
        for stage in range(4):
            for way in (UP, DOWN):
                x_copy(h, stage, way).wait_send()
    store_wg.wait()
    store_ig.wait()
    store_out.wait()


def finish(out_in, ig_in, wg_in, out_hbm, ig_hbm, wg_hbm, OUT, IG, WG, sem):
    rows = WG.shape[0] // 4
    moves = [(wg_in.at[pl.ds(i * rows, rows)], WG.at[pl.ds(i * rows, rows)], wg_hbm.at[pl.ds(i * rows, rows)]) for i in range(4)]
    moves += [(out_in, OUT, out_hbm), (ig_in, IG, ig_hbm)]
    loads = [pltpu.make_async_copy(a, b, sem.at[0, i]) for i, (a, b, _) in enumerate(moves)]
    stores = [pltpu.make_async_copy(b, c, sem.at[1, i]) for i, (_, b, c) in enumerate(moves)]
    for load in loads:
        load.start()
    for load, store in zip(loads, stores):
        load.wait()
        store.start()
    for store in stores:
        store.wait()


def local(inputs, weight, mask, cotangent):
    tok, depth = inputs.shape
    width = weight.shape[1]
    half = tok // 2
    steps = NZ // 2 + 1
    dma = pltpu.SemaphoreType.DMA
    hbm = pl.BlockSpec(memory_space=pl.ANY)
    tokens = tok * NC
    results = pl.pallas_call(
        functools.partial(kernel, float(tokens) ** -0.5),
        out_shape=(
            jax.ShapeDtypeStruct((tok, width), BF16),
            jax.ShapeDtypeStruct((tok, depth), BF16),
            jax.ShapeDtypeStruct((depth, width), BF16),
        ),
        in_specs=[hbm, hbm, pl.BlockSpec(memory_space=pltpu.SMEM), hbm],
        out_specs=(hbm, hbm, hbm),
        scratch_shapes=[
            pltpu.VMEM((4, 4, tok, depth), BF16),
            pltpu.VMEM((depth, tokens), BF16),
            pltpu.VMEM((depth, width), BF16),
            pltpu.VMEM((width, depth), BF16),
            pltpu.VMEM((tokens, width), BF16),
            pltpu.VMEM((NZ, tok, width), F32),
            pltpu.VMEM((NZ, tok, width), BF16),
            pltpu.VMEM((NZ, tok, width), BF16),
            pltpu.VMEM((2, 2, steps, half, width), BF16),
            pltpu.VMEM((2, 2, steps, half, width), BF16),
            pltpu.VMEM((NZ, 2, tok, depth), BF16),
            pltpu.VMEM((NC, tok, depth), BF16),
            pltpu.VMEM((depth, width), BF16),
            pltpu.VMEM((tok, width), BF16),
            pltpu.VMEM((tok, depth), BF16),
            dma((3,)),
            dma((2, 4, 2)), dma((2, 4, 2)),
            dma((2, 2, steps)), dma((2, 2, steps)),
            dma((NZ, 2)), dma((NZ, 2)),
            dma((NZ,)), dma((NZ,)),
            dma((2, 2, steps)), dma((2, 2, steps)),
            dma((NZ, 2)), dma((NC,)),
            dma((3,)),
        ],
        compiler_params=pltpu.CompilerParams(
            collective_id=0, has_side_effects=True, vmem_limit_bytes=60 * 1024 * 1024
        ),
        cost_estimate=pl.CostEstimate(
            flops=6 * tokens * depth * width, bytes_accessed=4 * depth * width + 4 * tok * (width + depth), transcendentals=0
        ),
    )(inputs, weight, mask, cotangent)
    return pl.pallas_call(
        finish,
        out_shape=tuple(jax.ShapeDtypeStruct(r.shape, r.dtype) for r in results),
        in_specs=[hbm] * 3,
        out_specs=(hbm,) * 3,
        scratch_shapes=[pltpu.VMEM(r.shape, r.dtype) for r in results] + [dma((2, 6))],
        compiler_params=pltpu.CompilerParams(vmem_limit_bytes=60 * 1024 * 1024),
    )(*results)


def solution(mesh):
    placed = (P("col", "row"), P("row", "col"), P("row", "col"), P("row", "col"))
    return jax.shard_map(
        local,
        mesh=mesh,
        in_specs=placed,
        out_specs=(P("row", "col"), P("col", "row"), P("row", "col")),
        check_vma=False,
    )
```

```python
import functools

import jax
import jax.numpy as jnp
from jax import lax
from jax.experimental import pallas as pl
from jax.experimental.pallas import tpu as pltpu
from jax.sharding import PartitionSpec as P

BLOCK = 128
NZ = 8
NC = 16
F32 = jnp.float32
BF16 = jnp.bfloat16
UP, DOWN = 0, 1


def remote(src, dst, send_sem, recv_sem, device):
    return pltpu.make_async_remote_copy(
        src_ref=src,
        dst_ref=dst,
        send_sem=send_sem,
        recv_sem=recv_sem,
        device_id=device,
        device_id_type=pl.DeviceIdType.MESH,
    )


def kernel(
    scale,
    x_hbm, w_hbm, mask_hbm, c_hbm,
    last_hbm, own_hbm, ig_hbm, wg_hbm,
    mask_smem, X, XT, W, WT, C, PO, PS_out, PS, S, R, G, GR, WG, IG,
    load_sem, x_send, x_recv, az_send, az_recv, as_send, as_recv,
    ps_send, ps_recv, r_send, r_recv, g_send, g_recv, store_sem,
):
    row = lax.axis_index("row")
    col = lax.axis_index("col")
    z, core = row // 2, row % 2
    tok, width = c_hbm.shape
    depth = x_hbm.shape[1]
    half = tok // 2
    up = ((row + 2) % (2 * NZ), col)
    down = ((row + 2 * NZ - 2) % (2 * NZ), col)
    sibling = (row + 1 - 2 * core, col)
    toward = (up, down)
    my_rows = core * tok

    cx, cy = col % 4, col // 4

    def step_x(n):
        return (row, cy * 4 + (cx + n + 4) % 4)

    def step_y(n):
        return (row, ((cy + n + 4) % 4) * 4 + cx)

    barrier = pltpu.get_barrier_semaphore()
    neighbours = (up, down, sibling, step_x(1), step_x(-1), step_y(1), step_y(-1))
    for device in neighbours:
        pl.semaphore_signal(barrier, inc=1, device_id=device, device_id_type=pl.DeviceIdType.MESH)

    load_c = pltpu.make_async_copy(c_hbm, C.at[pl.ds(my_rows, tok)], load_sem.at[0])
    load_x = pltpu.make_async_copy(x_hbm, X.at[cy, cx], load_sem.at[1])
    load_w = pltpu.make_async_copy(w_hbm, W, load_sem.at[2])
    load_c.start()
    load_x.start()
    load_w.start()
    load_mask = pltpu.make_async_copy(mask_hbm, mask_smem, load_sem.at[3])
    load_mask.start()

    pl.semaphore_wait(barrier, len(neighbours))

    def chunk(rel, part, owner=core):
        return C.at[pl.ds(rel * 2 * tok + owner * tok + part * half, half)]

    def gather_copy(way, part, dist):
        rel = (-dist if way == UP else dist) % NZ
        land = (rel - 1 if way == UP else rel + 1) % NZ
        src = c_hbm.at[pl.ds(part * half, half)] if dist == 0 else chunk(rel, part)
        return remote(src, chunk(land, part), az_send.at[way, part, dist], az_recv.at[way, part, dist], toward[way])

    def share_copy(rel, part):
        return remote(chunk(rel, part), chunk(rel, part), as_send.at[rel, part], as_recv.at[rel, part], sibling)

    def share_wait(rel):
        for part in range(2):
            other = chunk(rel, part, 1 - core)
            remote(other, other, as_send.at[rel, part], as_recv.at[rel, part], sibling).wait_recv()

    def last(way, part):
        return NZ // 2 if part == way else NZ // 2 - 1

    quarter = half // 2

    def x_copy(h, stage, way):
        sign = 1 if way == UP else -1
        step = (step_x if (h == 0) == (stage < 2) else step_y)(sign)
        back = 0 if stage % 2 == 0 else -sign
        rows = pl.ds(h * half, half) if stage % 2 == 0 else pl.ds(h * half + way * quarter, quarter)
        if stage < 2:
            xs, ys = ((cx + back + 4) % 4, cy) if h == 0 else (cx, (cy + back + 4) % 4)
            block = X.at[ys, xs, rows]
        elif h == 0:
            block = X.at[(cy + back + 4) % 4, :, rows]
        else:
            block = X.at[:, (cx + back + 4) % 4, rows]
        src = x_hbm.at[rows] if stage == 0 else block
        return remote(src, block, x_send.at[h, stage, way], x_recv.at[h, stage, way], step)

    def x_stage(stage):
        for h in range(2):
            for way in (UP, DOWN):
                if stage % 2 == 1:
                    x_copy(h, stage - 1, way).wait_recv()
                    x_copy(h, stage, way).start()
            if stage % 2 == 0:
                for way in (UP, DOWN):
                    if stage:
                        x_copy(h, stage - 1, way).wait_recv()
                for way in (UP, DOWN):
                    if stage < 4:
                        x_copy(h, stage, way).start()

    for way in (UP, DOWN):
        gather_copy(way, 0, 0).start()
    x_stage(0)
    for way in (UP, DOWN):
        gather_copy(way, 1, 0).start()
    load_c.wait()
    load_x.wait()
    for part in range(2):
        share_copy(0, part).start()

    load_w.wait()
    load_mask.wait()
    rows_w, cols_w = depth // BLOCK, width // BLOCK

    def mask_rows(i, carry):
        at = pl.ds(pl.multiple_of(i * BLOCK, BLOCK), BLOCK)
        for j in range(cols_w):
            to = pl.ds(j * BLOCK, BLOCK)
            keep = mask_smem[i, j].astype(F32)
            W[at, to] = (W[at, to].astype(F32) * keep).astype(BF16)
        return carry

    lax.fori_loop(0, rows_w, mask_rows, 0)

    def flip(j, carry):
        at = pl.ds(pl.multiple_of(j * 256, 256), 256)
        WT[at, :] = W[:, at].T
        return carry

    lax.fori_loop(0, width // 256, flip, 0)

    def gather_step(dist, lead):
        for way in (UP, DOWN):
            part = way if lead else 1 - way
            gather_copy(way, part, dist - 1).wait_recv()
            if dist < last(way, part):
                gather_copy(way, part, dist).start()
            rel = (-dist if way == UP else dist) % NZ
            share_copy(rel, part).start()

    def grad_partial(rel):
        share_wait(rel)
        value = jnp.dot(C[pl.ds(rel * 2 * tok, 2 * tok), :], WT[...], preferred_element_type=F32).astype(BF16)
        there = 2 * ((z + rel) % NZ)
        for owner in range(2):
            dest = there + owner
            G[rel, owner] = value[owner * tok:(owner + 1) * tok]

            @pl.when(dest == col)
            def _():
                GR[dest] = G[rel, owner]

            @pl.when(dest != col)
            def _():
                remote(G.at[rel, owner], GR.at[col], g_send.at[rel, owner], g_recv.at[col], (row, dest)).start()

    def product(rel):
        there = (z + rel) % NZ
        x_pair = X[there // 2, pl.ds(2 * (there % 2), 2)].reshape(2 * tok, depth)
        XT[:, pl.ds(rel * 2 * tok, 2 * tok)] = x_pair.T

        def column(n, carry):
            at = pl.ds(pl.multiple_of(n * 256, 256), 256)
            value = jnp.dot(x_pair, W[:, at], preferred_element_type=F32)
            first, second = value[:tok], value[tok:]
            PO[rel, :, at] = jnp.where(core == 0, first, second)
            PS_out[rel, :, at] = jnp.where(core == 0, second, first).astype(BF16)
            return carry

        lax.fori_loop(0, width // 256, column, 0)
        pair_copy(rel).start()

    def pair_copy(rel):
        return remote(PS_out.at[rel], PS.at[rel], ps_send.at[rel], ps_recv.at[rel], sibling)

    def reduce_copy(way, part, dist):
        land = last_hbm.at[way, pl.ds(part * half, half)] if dist == 1 else R.at[way, part, dist]
        return remote(S.at[way, part, dist], land, r_send.at[way, part, dist], r_recv.at[way, part, dist], toward[way])

    def reduce_send(way, part, dist):
        rel = (dist if way == UP else -dist) % NZ
        at = pl.ds(part * half, half)
        total = PO[rel, at, :] + PS[rel, at, :].astype(F32)
        if dist < last(way, part):
            reduce_copy(way, part, dist + 1).wait_recv()
            total += R[way, part, dist + 1].astype(F32)
        S[way, part, dist] = total.astype(BF16)
        reduce_copy(way, part, dist).start()

    def reduce_step(step, lead):
        for way in (UP, DOWN):
            part = way if lead else 1 - way
            reduce_send(way, part, last(way, part) - step)

    def weight_grad(n, carry):
        at = pl.ds(pl.multiple_of(n * 256, 256), 256)
        value = jnp.dot(XT[...], C[:, at], preferred_element_type=F32)
        for i in range(rows_w):
            for j in range(2):
                keep = mask_smem[i, n * 2 + j].astype(F32) * scale
                piece = value[i * BLOCK:(i + 1) * BLOCK, j * BLOCK:(j + 1) * BLOCK] * keep
                WG[pl.ds(i * BLOCK, BLOCK), pl.ds(pl.multiple_of(n * 256 + j * BLOCK, BLOCK), BLOCK)] = piece.astype(BF16)
        return carry

    x_stage(1)
    x_stage(2)
    gather_step(1, True)
    gather_step(1, False)
    x_stage(3)
    gather_step(2, True)
    x_stage(4)
    for rel in (4, 3, 5):
        product(rel)
    grad_partial(0)
    gather_step(2, False)
    for rel in (2, 6):
        product(rel)
    grad_partial(1)
    grad_partial(7)
    gather_step(3, True)
    for rel in (1, 7, 0):
        product(rel)
    for rel in (4, 3, 5):
        pair_copy(rel).wait_recv()
    reduce_step(0, True)
    reduce_step(0, False)
    grad_partial(2)
    grad_partial(6)
    gather_step(3, False)
    grad_partial(3)
    grad_partial(5)
    gather_step(4, True)
    grad_partial(4)
    for rel in (2, 6, 1, 7, 0):
        pair_copy(rel).wait_recv()
    reduce_step(1, True)
    lax.fori_loop(0, 2, weight_grad, 0)
    reduce_step(1, False)
    lax.fori_loop(2, 4, weight_grad, 0)
    reduce_step(2, True)
    lax.fori_loop(4, 6, weight_grad, 0)
    reduce_step(2, False)
    lax.fori_loop(6, width // 256, weight_grad, 0)
    store_wg = pltpu.make_async_copy(WG, wg_hbm, store_sem.at[0])
    store_wg.start()
    reduce_step(3, True)

    PO[0] = PO[0] + PS[0].astype(F32)
    store_own = pltpu.make_async_copy(PO.at[0], own_hbm, store_sem.at[2])
    store_own.start()

    def g_wait(j, carry):
        other = (col + j) % NC
        remote(GR.at[other], GR.at[other], g_send.at[0, 0], g_recv.at[other], (row, other)).wait_recv()
        return carry

    lax.fori_loop(1, NC, g_wait, 0)

    def g_sum(i, carry):
        at = pl.ds(pl.multiple_of(i * 16, 16), 16)
        total = GR[0, at, :].astype(F32)
        for c in range(1, NC):
            total += GR[c, at, :].astype(F32)
        IG[at, :] = total.astype(BF16)
        return carry

    lax.fori_loop(0, tok // 16, g_sum, 0)
    store_ig = pltpu.make_async_copy(IG, ig_hbm, store_sem.at[1])
    store_ig.start()

    for part in range(2):
        for way in (UP, DOWN):
            for dist in range(last(way, part)):
                gather_copy(way, part, dist).wait_send()
                if dist:
                    reduce_copy(way, part, dist + 1).wait_send()
        for rel in range(NZ):
            share_copy(rel, part).wait_send()
    for rel in range(NZ):
        pair_copy(rel).wait_send()
        for owner in range(2):
            dest = 2 * ((z + rel) % NZ) + owner

            @pl.when(dest != col)
            def _():
                remote(G.at[rel, owner], GR.at[col], g_send.at[rel, owner], g_recv.at[col], (row, dest)).wait_send()

    for h in range(2):
        for stage in range(4):
            for way in (UP, DOWN):
                x_copy(h, stage, way).wait_send()
    store_wg.wait()
    store_ig.wait()
    store_own.wait()
    for part in range(2):
        for way in (UP, DOWN):
            reduce_copy(way, part, 1).wait_recv()
            reduce_copy(way, part, 1).wait_send()


def finish(last, own, ig_in, wg_in, out_hbm, ig_hbm, wg_hbm, OUT, sem):
    store_wg = pltpu.make_async_copy(wg_in, wg_hbm, sem.at[0])
    store_ig = pltpu.make_async_copy(ig_in, ig_hbm, sem.at[1])
    store_wg.start()
    store_ig.start()
    half = OUT.shape[0] // 2
    stores = []
    for part in range(2):
        at = pl.ds(part * half, half)
        OUT[at] = (own[at] + last[UP, at].astype(F32) + last[DOWN, at].astype(F32)).astype(BF16)
        stores.append(pltpu.make_async_copy(OUT.at[at], out_hbm.at[at], sem.at[2 + part]))
        stores[part].start()
    for store in [store_wg, store_ig] + stores:
        store.wait()


def local(inputs, weight, mask, cotangent):
    tok, depth = inputs.shape
    width = weight.shape[1]
    half = tok // 2
    steps = NZ // 2 + 1
    dma = pltpu.SemaphoreType.DMA
    hbm = pl.BlockSpec(memory_space=pl.ANY)
    tokens = tok * NC
    results = pl.pallas_call(
        functools.partial(kernel, float(tokens) ** -0.5),
        out_shape=(
            jax.ShapeDtypeStruct((2, tok, width), BF16),
            jax.ShapeDtypeStruct((tok, width), F32),
            jax.ShapeDtypeStruct((tok, depth), BF16),
            jax.ShapeDtypeStruct((depth, width), BF16),
        ),
        in_specs=[hbm] * 4,
        out_specs=(hbm,) * 4,
        scratch_shapes=[
            pltpu.SMEM(mask.shape, mask.dtype),
            pltpu.VMEM((4, 4, tok, depth), BF16),
            pltpu.VMEM((depth, tokens), BF16),
            pltpu.VMEM((depth, width), BF16),
            pltpu.VMEM((width, depth), BF16),
            pltpu.VMEM((tokens, width), BF16),
            pltpu.VMEM((NZ, tok, width), F32),
            pltpu.VMEM((NZ, tok, width), BF16),
            pltpu.VMEM((NZ, tok, width), BF16),
            pltpu.VMEM((2, 2, steps, half, width), BF16),
            pltpu.VMEM((2, 2, steps, half, width), BF16),
            pltpu.VMEM((NZ, 2, tok, depth), BF16),
            pltpu.VMEM((NC, tok, depth), BF16),
            pltpu.VMEM((depth, width), BF16),
            pltpu.VMEM((tok, depth), BF16),
            dma((4,)),
            dma((2, 4, 2)), dma((2, 4, 2)),
            dma((2, 2, steps)), dma((2, 2, steps)),
            dma((NZ, 2)), dma((NZ, 2)),
            dma((NZ,)), dma((NZ,)),
            dma((2, 2, steps)), dma((2, 2, steps)),
            dma((NZ, 2)), dma((NC,)),
            dma((3,)),
        ],
        compiler_params=pltpu.CompilerParams(
            collective_id=0, has_side_effects=True, vmem_limit_bytes=44 * 1024 * 1024
        ),
        cost_estimate=pl.CostEstimate(
            flops=6 * tokens * depth * width, bytes_accessed=4 * depth * width + 4 * tok * (width + depth), transcendentals=0
        ),
    )(*(pltpu.with_memory_space_constraint(a, pltpu.HBM) for a in (inputs, weight, mask, cotangent)))
    shapes = ((tok, width), (tok, depth), (depth, width))
    return pl.pallas_call(
        finish,
        out_shape=tuple(jax.ShapeDtypeStruct(shape, BF16) for shape in shapes),
        in_specs=[pl.BlockSpec(memory_space=pltpu.VMEM)] * 4,
        out_specs=(hbm,) * 3,
        scratch_shapes=[pltpu.VMEM((tok, width), BF16), dma((4,))],
        compiler_params=pltpu.CompilerParams(vmem_limit_bytes=8 * 1024 * 1024),
    )(*results)


def solution(mesh):
    placed = (P("col", "row"), P("row", "col"), P("row", "col"), P("row", "col"))
    return jax.shard_map(
        local,
        mesh=mesh,
        in_specs=placed,
        out_specs=(P("row", "col"), P("col", "row"), P("row", "col")),
        check_vma=False,
    )
```

```python
import functools

import jax
import jax.numpy as jnp
from jax import lax
from jax.experimental import pallas as pl
from jax.experimental.pallas import tpu as pltpu
from jax.sharding import PartitionSpec as P

BLOCK = 128
NZ = 8
NC = 16
F32 = jnp.float32
BF16 = jnp.bfloat16
UP, DOWN = 0, 1


def remote(src, dst, send_sem, recv_sem, device):
    return pltpu.make_async_remote_copy(
        src_ref=src,
        dst_ref=dst,
        send_sem=send_sem,
        recv_sem=recv_sem,
        device_id=device,
        device_id_type=pl.DeviceIdType.MESH,
    )


def kernel(
    scale,
    x_hbm, w_hbm, mask_hbm, c_hbm,
    last_hbm, own_hbm, ig_hbm, wg_hbm,
    mask_smem, X, XT, W, WT, C, PO, PS_out, PS, S, R, G, GR, WG, IG,
    load_sem, x_send, x_recv, az_send, az_recv, as_send, as_recv,
    ps_send, ps_recv, r_send, r_recv, g_send, g_recv, store_sem,
):
    row = lax.axis_index("row")
    col = lax.axis_index("col")
    z, core = row // 2, row % 2
    tok, width = c_hbm.shape
    depth = x_hbm.shape[1]
    half = tok // 2
    up = ((row + 2) % (2 * NZ), col)
    down = ((row + 2 * NZ - 2) % (2 * NZ), col)
    sibling = (row + 1 - 2 * core, col)
    toward = (up, down)
    my_rows = core * tok

    cx, cy = col % 4, col // 4

    def step_x(n):
        return (row, cy * 4 + (cx + n + 4) % 4)

    def step_y(n):
        return (row, ((cy + n + 4) % 4) * 4 + cx)

    barrier = pltpu.get_barrier_semaphore()
    neighbours = (step_x(1), step_x(-1), step_y(1), step_y(-1), up, down, sibling)
    for device in neighbours:
        pl.semaphore_signal(barrier, inc=1, device_id=device, device_id_type=pl.DeviceIdType.MESH)

    load_c = pltpu.make_async_copy(c_hbm, C.at[pl.ds(my_rows, tok)], load_sem.at[0])
    load_x = pltpu.make_async_copy(x_hbm, X.at[cy, cx], load_sem.at[1])
    load_w = pltpu.make_async_copy(w_hbm, W, load_sem.at[2])
    load_mask = pltpu.make_async_copy(mask_hbm, mask_smem, load_sem.at[3])
    pl.semaphore_wait(barrier, len(neighbours))

    def chunk(rel, part, owner=core):
        return C.at[pl.ds(rel * 2 * tok + owner * tok + part * half, half)]

    def gather_copy(way, part, dist):
        rel = (-dist if way == UP else dist) % NZ
        land = (rel - 1 if way == UP else rel + 1) % NZ
        src = c_hbm.at[pl.ds(part * half, half)] if dist == 0 else chunk(rel, part)
        return remote(src, chunk(land, part), az_send.at[way, part, dist], az_recv.at[way, part, dist], toward[way])

    def share_copy(rel, part):
        return remote(chunk(rel, part), chunk(rel, part), as_send.at[rel, part], as_recv.at[rel, part], sibling)

    def share_wait(rel):
        for part in range(2):
            other = chunk(rel, part, 1 - core)
            remote(other, other, as_send.at[rel, part], as_recv.at[rel, part], sibling).wait_recv()

    def last(way, part):
        return NZ // 2 if part == way else NZ // 2 - 1

    quarter = half // 2

    def x_copy(h, stage, way):
        sign = 1 if way == UP else -1
        step = (step_x if (h == 0) == (stage < 2) else step_y)(sign)
        back = 0 if stage % 2 == 0 else -sign
        rows = pl.ds(h * half, half) if stage % 2 == 0 else pl.ds(h * half + way * quarter, quarter)
        if stage < 2:
            xs, ys = ((cx + back + 4) % 4, cy) if h == 0 else (cx, (cy + back + 4) % 4)
            block = X.at[ys, xs, rows]
        elif h == 0:
            block = X.at[(cy + back + 4) % 4, :, rows]
        else:
            block = X.at[:, (cx + back + 4) % 4, rows]
        src = x_hbm.at[rows] if stage == 0 else block
        return remote(src, block, x_send.at[h, stage, way], x_recv.at[h, stage, way], step)

    def x_stage(stage):
        for h in range(2):
            for way in (UP, DOWN):
                if stage % 2 == 1:
                    x_copy(h, stage - 1, way).wait_recv()
                    x_copy(h, stage, way).start()
            if stage % 2 == 0:
                for way in (UP, DOWN):
                    if stage:
                        x_copy(h, stage - 1, way).wait_recv()
                for way in (UP, DOWN):
                    if stage < 4:
                        x_copy(h, stage, way).start()

    for way in (UP, DOWN):
        gather_copy(way, 0, 0).start()
    x_stage(0)
    for way in (UP, DOWN):
        gather_copy(way, 1, 0).start()
    for load in (load_c, load_x, load_w, load_mask):
        load.start()
    load_c.wait()
    load_x.wait()
    for part in range(2):
        share_copy(0, part).start()

    load_w.wait()
    load_mask.wait()
    rows_w, cols_w = depth // BLOCK, width // BLOCK

    def mask_rows(i, carry):
        at = pl.ds(pl.multiple_of(i * BLOCK, BLOCK), BLOCK)
        for j in range(cols_w):
            to = pl.ds(j * BLOCK, BLOCK)
            keep = mask_smem[i, j].astype(F32)
            W[at, to] = (W[at, to].astype(F32) * keep).astype(BF16)
        return carry

    lax.fori_loop(0, rows_w, mask_rows, 0)

    def flip(j, carry):
        at = pl.ds(pl.multiple_of(j * 256, 256), 256)
        WT[at, :] = W[:, at].T
        return carry

    lax.fori_loop(0, width // 256, flip, 0)

    def gather_step(dist, lead):
        for way in (UP, DOWN):
            part = way if lead else 1 - way
            gather_copy(way, part, dist - 1).wait_recv()
            if dist < last(way, part):
                gather_copy(way, part, dist).start()
            rel = (-dist if way == UP else dist) % NZ
            share_copy(rel, part).start()

    def grad_partial(rel):
        share_wait(rel)
        value = jnp.dot(C[pl.ds(rel * 2 * tok, 2 * tok), :], WT[...], preferred_element_type=F32).astype(BF16)
        there = 2 * ((z + rel) % NZ)
        for owner in range(2):
            dest = there + owner
            G[rel, owner] = value[owner * tok:(owner + 1) * tok]

            @pl.when(dest == col)
            def _():
                GR[dest] = G[rel, owner]

            @pl.when(dest != col)
            def _():
                remote(G.at[rel, owner], GR.at[col], g_send.at[rel, owner], g_recv.at[col], (row, dest)).start()

    def product(rel):
        there = (z + rel) % NZ
        x_pair = X[there // 2, pl.ds(2 * (there % 2), 2)].reshape(2 * tok, depth)
        XT[:, pl.ds(rel * 2 * tok, 2 * tok)] = x_pair.T

        def column(n, carry):
            at = pl.ds(pl.multiple_of(n * 256, 256), 256)
            value = jnp.dot(x_pair, W[:, at], preferred_element_type=F32)
            first, second = value[:tok], value[tok:]
            PO[rel, :, at] = jnp.where(core == 0, first, second)
            PS_out[rel, :, at] = jnp.where(core == 0, second, first).astype(BF16)
            return carry

        lax.fori_loop(0, width // 256, column, 0)
        pair_copy(rel).start()

    def pair_copy(rel):
        return remote(PS_out.at[rel], PS.at[rel], ps_send.at[rel], ps_recv.at[rel], sibling)

    def reduce_copy(way, part, dist):
        land = last_hbm.at[way, pl.ds(part * half, half)] if dist == 1 else R.at[way, part, dist]
        return remote(S.at[way, part, dist], land, r_send.at[way, part, dist], r_recv.at[way, part, dist], toward[way])

    def reduce_send(way, part, dist):
        rel = (dist if way == UP else -dist) % NZ
        at = pl.ds(part * half, half)
        total = PO[rel, at, :] + PS[rel, at, :].astype(F32)
        if dist < last(way, part):
            reduce_copy(way, part, dist + 1).wait_recv()
            total += R[way, part, dist + 1].astype(F32)
        S[way, part, dist] = total.astype(BF16)
        reduce_copy(way, part, dist).start()

    def reduce_step(step, lead):
        for way in (UP, DOWN):
            part = way if lead else 1 - way
            reduce_send(way, part, last(way, part) - step)

    def weight_grad(n, carry):
        at = pl.ds(pl.multiple_of(n * 256, 256), 256)
        value = jnp.dot(XT[...], C[:, at], preferred_element_type=F32)
        for i in range(rows_w):
            for j in range(2):
                keep = mask_smem[i, n * 2 + j].astype(F32) * scale
                piece = value[i * BLOCK:(i + 1) * BLOCK, j * BLOCK:(j + 1) * BLOCK] * keep
                WG[pl.ds(i * BLOCK, BLOCK), pl.ds(pl.multiple_of(n * 256 + j * BLOCK, BLOCK), BLOCK)] = piece.astype(BF16)
        return carry

    x_stage(1)
    x_stage(2)
    gather_step(1, True)
    gather_step(1, False)
    x_stage(3)
    gather_step(2, True)
    x_stage(4)
    for rel in (4, 3, 5):
        product(rel)
    grad_partial(0)
    gather_step(2, False)
    for rel in (2, 6):
        product(rel)
    grad_partial(1)
    grad_partial(7)
    gather_step(3, True)
    for rel in (1, 7, 0):
        product(rel)
    for rel in (4, 3, 5):
        pair_copy(rel).wait_recv()
    reduce_step(0, True)
    reduce_step(0, False)
    grad_partial(2)
    grad_partial(6)
    gather_step(3, False)
    grad_partial(3)
    grad_partial(5)
    gather_step(4, True)
    grad_partial(4)
    for rel in (2, 6, 1, 7, 0):
        pair_copy(rel).wait_recv()
    reduce_step(1, True)
    lax.fori_loop(0, 2, weight_grad, 0)
    reduce_step(1, False)
    lax.fori_loop(2, 4, weight_grad, 0)
    reduce_step(2, True)
    lax.fori_loop(4, 6, weight_grad, 0)
    reduce_step(2, False)
    lax.fori_loop(6, width // 256, weight_grad, 0)
    store_wg = pltpu.make_async_copy(WG, wg_hbm, store_sem.at[0])
    store_wg.start()
    reduce_step(3, True)

    PO[0] = PO[0] + PS[0].astype(F32)
    store_own = pltpu.make_async_copy(PO.at[0], own_hbm, store_sem.at[2])
    store_own.start()

    def g_wait(j, carry):
        other = (col + j) % NC
        remote(GR.at[other], GR.at[other], g_send.at[0, 0], g_recv.at[other], (row, other)).wait_recv()
        return carry

    lax.fori_loop(1, NC, g_wait, 0)

    def g_sum(i, carry):
        at = pl.ds(pl.multiple_of(i * 16, 16), 16)
        total = GR[0, at, :].astype(F32)
        for c in range(1, NC):
            total += GR[c, at, :].astype(F32)
        IG[at, :] = total.astype(BF16)
        return carry

    lax.fori_loop(0, tok // 16, g_sum, 0)
    store_ig = pltpu.make_async_copy(IG, ig_hbm, store_sem.at[1])
    store_ig.start()

    for part in range(2):
        for way in (UP, DOWN):
            for dist in range(last(way, part)):
                gather_copy(way, part, dist).wait_send()
                if dist:
                    reduce_copy(way, part, dist + 1).wait_send()
        for rel in range(NZ):
            share_copy(rel, part).wait_send()
    for rel in range(NZ):
        pair_copy(rel).wait_send()
        for owner in range(2):
            dest = 2 * ((z + rel) % NZ) + owner

            @pl.when(dest != col)
            def _():
                remote(G.at[rel, owner], GR.at[col], g_send.at[rel, owner], g_recv.at[col], (row, dest)).wait_send()

    for h in range(2):
        for stage in range(4):
            for way in (UP, DOWN):
                x_copy(h, stage, way).wait_send()
    store_wg.wait()
    store_ig.wait()
    store_own.wait()
    for part in range(2):
        for way in (UP, DOWN):
            reduce_copy(way, part, 1).wait_recv()
            reduce_copy(way, part, 1).wait_send()


def finish(last, own, ig_in, wg_in, out_hbm, ig_hbm, wg_hbm, OUT, sem):
    rows = wg_in.shape[0] // 4
    stores = [pltpu.make_async_copy(wg_in.at[pl.ds(i * rows, rows)], wg_hbm.at[pl.ds(i * rows, rows)], sem.at[2 + i]) for i in range(4)]
    stores.append(pltpu.make_async_copy(ig_in, ig_hbm, sem.at[6]))
    for store in stores:
        store.start()
    half = OUT.shape[0] // 2
    for part in range(2):
        at = pl.ds(part * half, half)
        OUT[at] = (own[at] + last[UP, at].astype(F32) + last[DOWN, at].astype(F32)).astype(BF16)
        stores.append(pltpu.make_async_copy(OUT.at[at], out_hbm.at[at], sem.at[part]))
        stores[-1].start()
    for store in stores:
        store.wait()


def local(inputs, weight, mask, cotangent):
    tok, depth = inputs.shape
    width = weight.shape[1]
    half = tok // 2
    steps = NZ // 2 + 1
    dma = pltpu.SemaphoreType.DMA
    hbm = pl.BlockSpec(memory_space=pl.ANY)
    tokens = tok * NC
    results = pl.pallas_call(
        functools.partial(kernel, float(tokens) ** -0.5),
        out_shape=(
            jax.ShapeDtypeStruct((2, tok, width), BF16),
            jax.ShapeDtypeStruct((tok, width), F32),
            jax.ShapeDtypeStruct((tok, depth), BF16),
            jax.ShapeDtypeStruct((depth, width), BF16),
        ),
        in_specs=[hbm] * 4,
        out_specs=(hbm,) * 4,
        scratch_shapes=[
            pltpu.SMEM(mask.shape, mask.dtype),
            pltpu.VMEM((4, 4, tok, depth), BF16),
            pltpu.VMEM((depth, tokens), BF16),
            pltpu.VMEM((depth, width), BF16),
            pltpu.VMEM((width, depth), BF16),
            pltpu.VMEM((tokens, width), BF16),
            pltpu.VMEM((NZ, tok, width), F32),
            pltpu.VMEM((NZ, tok, width), BF16),
            pltpu.VMEM((NZ, tok, width), BF16),
            pltpu.VMEM((2, 2, steps, half, width), BF16),
            pltpu.VMEM((2, 2, steps, half, width), BF16),
            pltpu.VMEM((NZ, 2, tok, depth), BF16),
            pltpu.VMEM((NC, tok, depth), BF16),
            pltpu.VMEM((depth, width), BF16),
            pltpu.VMEM((tok, depth), BF16),
            dma((4,)),
            dma((2, 4, 2)), dma((2, 4, 2)),
            dma((2, 2, steps)), dma((2, 2, steps)),
            dma((NZ, 2)), dma((NZ, 2)),
            dma((NZ,)), dma((NZ,)),
            dma((2, 2, steps)), dma((2, 2, steps)),
            dma((NZ, 2)), dma((NC,)),
            dma((3,)),
        ],
        compiler_params=pltpu.CompilerParams(
            collective_id=0, has_side_effects=True, vmem_limit_bytes=44 * 1024 * 1024
        ),
        cost_estimate=pl.CostEstimate(
            flops=6 * tokens * depth * width, bytes_accessed=4 * depth * width + 4 * tok * (width + depth), transcendentals=0
        ),
    )(*(pltpu.with_memory_space_constraint(a, pltpu.HBM) for a in (inputs, weight, mask, cotangent)))
    shapes = ((tok, width), (tok, depth), (depth, width))
    return pl.pallas_call(
        finish,
        out_shape=tuple(jax.ShapeDtypeStruct(shape, BF16) for shape in shapes),
        in_specs=[pl.BlockSpec(memory_space=pltpu.VMEM)] * 4,
        out_specs=(hbm,) * 3,
        scratch_shapes=[pltpu.VMEM((tok, width), BF16), dma((7,))],
        compiler_params=pltpu.CompilerParams(vmem_limit_bytes=8 * 1024 * 1024),
    )(*results)


def solution(mesh):
    placed = (P("col", "row"), P("row", "col"), P("row", "col"), P("row", "col"))
    return jax.shard_map(
        local,
        mesh=mesh,
        in_specs=placed,
        out_specs=(P("row", "col"), P("col", "row"), P("row", "col")),
        check_vma=False,
    )
```

```python
import functools

import jax
import jax.numpy as jnp
from jax import lax
from jax.experimental import pallas as pl
from jax.experimental.pallas import tpu as pltpu
from jax.sharding import PartitionSpec as P

BLOCK = 128
NZ = 8
NC = 16
F32 = jnp.float32
BF16 = jnp.bfloat16
UP, DOWN = 0, 1


def remote(src, dst, send_sem, recv_sem, device):
    return pltpu.make_async_remote_copy(
        src_ref=src,
        dst_ref=dst,
        send_sem=send_sem,
        recv_sem=recv_sem,
        device_id=device,
        device_id_type=pl.DeviceIdType.MESH,
    )


def kernel(
    scale,
    x_hbm, w_hbm, mask_hbm, c_hbm,
    last_hbm, own_hbm, ig_hbm, wg_hbm,
    mask_smem, X, XT, W, WT, C, PO, PS_out, PS, S, R, G, GR, WG, IG,
    load_sem, x_send, x_recv, az_send, az_recv, as_send, as_recv,
    ps_send, ps_recv, r_send, r_recv, g_send, g_recv, store_sem,
):
    row = lax.axis_index("row")
    col = lax.axis_index("col")
    z, core = row // 2, row % 2
    tok, width = c_hbm.shape
    depth = x_hbm.shape[1]
    half = tok // 2
    up = ((row + 2) % (2 * NZ), col)
    down = ((row + 2 * NZ - 2) % (2 * NZ), col)
    sibling = (row + 1 - 2 * core, col)
    toward = (up, down)
    my_rows = core * tok

    cx, cy = col % 4, col // 4

    def step_x(n):
        return (row, cy * 4 + (cx + n + 4) % 4)

    def step_y(n):
        return (row, ((cy + n + 4) % 4) * 4 + cx)

    barrier = pltpu.get_barrier_semaphore()
    neighbours = (step_x(1), step_x(-1), step_y(1), step_y(-1), up, down, sibling)
    for device in neighbours:
        pl.semaphore_signal(barrier, inc=1, device_id=device, device_id_type=pl.DeviceIdType.MESH)

    load_c = pltpu.make_async_copy(c_hbm, C.at[pl.ds(my_rows, tok)], load_sem.at[0])
    load_x = pltpu.make_async_copy(x_hbm, X.at[cy, cx], load_sem.at[1])
    load_w = pltpu.make_async_copy(w_hbm, W, load_sem.at[2])
    load_mask = pltpu.make_async_copy(mask_hbm, mask_smem, load_sem.at[3])
    pl.semaphore_wait(barrier, len(neighbours))

    def chunk(rel, part, owner=core):
        return C.at[pl.ds(rel * 2 * tok + owner * tok + part * half, half)]

    def gather_copy(way, part, dist):
        rel = (-dist if way == UP else dist) % NZ
        land = (rel - 1 if way == UP else rel + 1) % NZ
        src = c_hbm.at[pl.ds(part * half, half)] if dist == 0 else chunk(rel, part)
        return remote(src, chunk(land, part), az_send.at[way, part, dist], az_recv.at[way, part, dist], toward[way])

    def share_copy(rel, part):
        return remote(chunk(rel, part), chunk(rel, part), as_send.at[rel, part], as_recv.at[rel, part], sibling)

    def share_wait(rel):
        for part in range(2):
            other = chunk(rel, part, 1 - core)
            remote(other, other, as_send.at[rel, part], as_recv.at[rel, part], sibling).wait_recv()

    def last(way, part):
        return NZ // 2 if part == way else NZ // 2 - 1

    quarter = half // 2

    def x_copy(h, stage, way):
        sign = 1 if way == UP else -1
        step = (step_x if (h == 0) == (stage < 2) else step_y)(sign)
        back = 0 if stage % 2 == 0 else -sign
        rows = pl.ds(h * half, half) if stage % 2 == 0 else pl.ds(h * half + way * quarter, quarter)
        if stage < 2:
            xs, ys = ((cx + back + 4) % 4, cy) if h == 0 else (cx, (cy + back + 4) % 4)
            block = X.at[ys, xs, rows]
        elif h == 0:
            block = X.at[(cy + back + 4) % 4, :, rows]
        else:
            block = X.at[:, (cx + back + 4) % 4, rows]
        src = x_hbm.at[rows] if stage == 0 else block
        return remote(src, block, x_send.at[h, stage, way], x_recv.at[h, stage, way], step)

    def x_stage(stage):
        for h in range(2):
            for way in (UP, DOWN):
                if stage % 2 == 1:
                    x_copy(h, stage - 1, way).wait_recv()
                    x_copy(h, stage, way).start()
            if stage % 2 == 0:
                for way in (UP, DOWN):
                    if stage:
                        x_copy(h, stage - 1, way).wait_recv()
                for way in (UP, DOWN):
                    if stage < 4:
                        x_copy(h, stage, way).start()

    x_stage(0)
    for way in (UP, DOWN):
        gather_copy(way, 0, 0).start()
    for way in (UP, DOWN):
        gather_copy(way, 1, 0).start()
    for load in (load_c, load_x, load_w, load_mask):
        load.start()
    load_c.wait()
    load_x.wait()
    for part in range(2):
        share_copy(0, part).start()

    load_w.wait()
    load_mask.wait()
    rows_w, cols_w = depth // BLOCK, width // BLOCK

    def mask_rows(i, carry):
        at = pl.ds(pl.multiple_of(i * BLOCK, BLOCK), BLOCK)
        for j in range(cols_w):
            to = pl.ds(j * BLOCK, BLOCK)
            keep = mask_smem[i, j].astype(F32)
            W[at, to] = (W[at, to].astype(F32) * keep).astype(BF16)
        return carry

    lax.fori_loop(0, rows_w, mask_rows, 0)

    def flip(j, carry):
        at = pl.ds(pl.multiple_of(j * 256, 256), 256)
        WT[at, :] = W[:, at].T
        return carry

    lax.fori_loop(0, width // 256, flip, 0)

    def gather_step(dist, lead):
        for way in (UP, DOWN):
            part = way if lead else 1 - way
            gather_copy(way, part, dist - 1).wait_recv()
            if dist < last(way, part):
                gather_copy(way, part, dist).start()
            rel = (-dist if way == UP else dist) % NZ
            share_copy(rel, part).start()

    def grad_partial(rel):
        share_wait(rel)
        value = jnp.dot(C[pl.ds(rel * 2 * tok, 2 * tok), :], WT[...], preferred_element_type=F32).astype(BF16)
        there = 2 * ((z + rel) % NZ)
        for owner in range(2):
            dest = there + owner
            G[rel, owner] = value[owner * tok:(owner + 1) * tok]

            @pl.when(dest == col)
            def _():
                GR[dest] = G[rel, owner]

            @pl.when(dest != col)
            def _():
                remote(G.at[rel, owner], GR.at[col], g_send.at[rel, owner], g_recv.at[col], (row, dest)).start()

    def product(rel):
        there = (z + rel) % NZ
        x_pair = X[there // 2, pl.ds(2 * (there % 2), 2)].reshape(2 * tok, depth)
        XT[:, pl.ds(rel * 2 * tok, 2 * tok)] = x_pair.T

        def column(n, carry):
            at = pl.ds(pl.multiple_of(n * 256, 256), 256)
            value = jnp.dot(x_pair, W[:, at], preferred_element_type=F32)
            first, second = value[:tok], value[tok:]
            PO[rel, :, at] = jnp.where(core == 0, first, second)
            PS_out[rel, :, at] = jnp.where(core == 0, second, first).astype(BF16)
            return carry

        lax.fori_loop(0, width // 256, column, 0)
        pair_copy(rel).start()

    def pair_copy(rel):
        return remote(PS_out.at[rel], PS.at[rel], ps_send.at[rel], ps_recv.at[rel], sibling)

    def reduce_copy(way, part, dist):
        land = last_hbm.at[way, pl.ds(part * half, half)] if dist == 1 else R.at[way, part, dist]
        return remote(S.at[way, part, dist], land, r_send.at[way, part, dist], r_recv.at[way, part, dist], toward[way])

    def reduce_send(way, part, dist):
        rel = (dist if way == UP else -dist) % NZ
        at = pl.ds(part * half, half)
        total = PO[rel, at, :] + PS[rel, at, :].astype(F32)
        if dist < last(way, part):
            reduce_copy(way, part, dist + 1).wait_recv()
            total += R[way, part, dist + 1].astype(F32)
        S[way, part, dist] = total.astype(BF16)
        reduce_copy(way, part, dist).start()

    def reduce_step(step, lead):
        for way in (UP, DOWN):
            part = way if lead else 1 - way
            reduce_send(way, part, last(way, part) - step)

    def weight_grad(n, carry):
        at = pl.ds(pl.multiple_of(n * 256, 256), 256)
        value = jnp.dot(XT[...], C[:, at], preferred_element_type=F32)
        for i in range(rows_w):
            for j in range(2):
                keep = mask_smem[i, n * 2 + j].astype(F32) * scale
                piece = value[i * BLOCK:(i + 1) * BLOCK, j * BLOCK:(j + 1) * BLOCK] * keep
                WG[pl.ds(i * BLOCK, BLOCK), pl.ds(pl.multiple_of(n * 256 + j * BLOCK, BLOCK), BLOCK)] = piece.astype(BF16)
        return carry

    x_stage(1)
    x_stage(2)
    gather_step(1, True)
    gather_step(1, False)
    x_stage(3)
    gather_step(2, True)
    x_stage(4)
    for rel in (4, 3, 5):
        product(rel)
    grad_partial(0)
    gather_step(2, False)
    for rel in (2, 6):
        product(rel)
    grad_partial(1)
    grad_partial(7)
    gather_step(3, True)
    for rel in (1, 7, 0):
        product(rel)
    for rel in (4, 3, 5):
        pair_copy(rel).wait_recv()
    reduce_step(0, True)
    reduce_step(0, False)
    grad_partial(2)
    grad_partial(6)
    gather_step(3, False)
    grad_partial(3)
    grad_partial(5)
    gather_step(4, True)
    grad_partial(4)
    for rel in (2, 6, 1, 7, 0):
        pair_copy(rel).wait_recv()
    reduce_step(1, True)
    lax.fori_loop(0, 2, weight_grad, 0)
    reduce_step(1, False)
    lax.fori_loop(2, 4, weight_grad, 0)
    reduce_step(2, True)
    lax.fori_loop(4, 6, weight_grad, 0)
    reduce_step(2, False)
    lax.fori_loop(6, width // 256, weight_grad, 0)
    store_wg = pltpu.make_async_copy(WG, wg_hbm, store_sem.at[0])
    store_wg.start()
    reduce_step(3, True)

    PO[0] = PO[0] + PS[0].astype(F32)
    store_own = pltpu.make_async_copy(PO.at[0], own_hbm, store_sem.at[2])
    store_own.start()

    def g_wait(j, carry):
        other = (col + j) % NC
        remote(GR.at[other], GR.at[other], g_send.at[0, 0], g_recv.at[other], (row, other)).wait_recv()
        return carry

    lax.fori_loop(1, NC, g_wait, 0)

    def g_sum(i, carry):
        at = pl.ds(pl.multiple_of(i * 16, 16), 16)
        total = GR[0, at, :].astype(F32)
        for c in range(1, NC):
            total += GR[c, at, :].astype(F32)
        IG[at, :] = total.astype(BF16)
        return carry

    lax.fori_loop(0, tok // 16, g_sum, 0)
    store_ig = pltpu.make_async_copy(IG, ig_hbm, store_sem.at[1])
    store_ig.start()

    for part in range(2):
        for way in (UP, DOWN):
            for dist in range(last(way, part)):
                gather_copy(way, part, dist).wait_send()
                if dist:
                    reduce_copy(way, part, dist + 1).wait_send()
        for rel in range(NZ):
            share_copy(rel, part).wait_send()
    for rel in range(NZ):
        pair_copy(rel).wait_send()
        for owner in range(2):
            dest = 2 * ((z + rel) % NZ) + owner

            @pl.when(dest != col)
            def _():
                remote(G.at[rel, owner], GR.at[col], g_send.at[rel, owner], g_recv.at[col], (row, dest)).wait_send()

    for h in range(2):
        for stage in range(4):
            for way in (UP, DOWN):
                x_copy(h, stage, way).wait_send()
    store_wg.wait()
    store_ig.wait()
    store_own.wait()
    for part in range(2):
        for way in (UP, DOWN):
            reduce_copy(way, part, 1).wait_recv()
            reduce_copy(way, part, 1).wait_send()


def finish(last, own, ig_in, wg_in, out_hbm, ig_hbm, wg_hbm, OUT, sem):
    rows = wg_in.shape[0] // 4
    stores = [pltpu.make_async_copy(wg_in.at[pl.ds(i * rows, rows)], wg_hbm.at[pl.ds(i * rows, rows)], sem.at[2 + i]) for i in range(4)]
    stores.append(pltpu.make_async_copy(ig_in, ig_hbm, sem.at[6]))
    for store in stores:
        store.start()
    half = OUT.shape[0] // 2
    for part in range(2):
        at = pl.ds(part * half, half)
        OUT[at] = (own[at] + last[UP, at].astype(F32) + last[DOWN, at].astype(F32)).astype(BF16)
        stores.append(pltpu.make_async_copy(OUT.at[at], out_hbm.at[at], sem.at[part]))
        stores[-1].start()
    for store in stores:
        store.wait()


def local(inputs, weight, mask, cotangent):
    tok, depth = inputs.shape
    width = weight.shape[1]
    half = tok // 2
    steps = NZ // 2 + 1
    dma = pltpu.SemaphoreType.DMA
    hbm = pl.BlockSpec(memory_space=pl.ANY)
    tokens = tok * NC
    results = pl.pallas_call(
        functools.partial(kernel, float(tokens) ** -0.5),
        out_shape=(
            jax.ShapeDtypeStruct((2, tok, width), BF16),
            jax.ShapeDtypeStruct((tok, width), F32),
            jax.ShapeDtypeStruct((tok, depth), BF16),
            jax.ShapeDtypeStruct((depth, width), BF16),
        ),
        in_specs=[hbm] * 4,
        out_specs=(hbm,) * 4,
        scratch_shapes=[
            pltpu.SMEM(mask.shape, mask.dtype),
            pltpu.VMEM((4, 4, tok, depth), BF16),
            pltpu.VMEM((depth, tokens), BF16),
            pltpu.VMEM((depth, width), BF16),
            pltpu.VMEM((width, depth), BF16),
            pltpu.VMEM((tokens, width), BF16),
            pltpu.VMEM((NZ, tok, width), F32),
            pltpu.VMEM((NZ, tok, width), BF16),
            pltpu.VMEM((NZ, tok, width), BF16),
            pltpu.VMEM((2, 2, steps, half, width), BF16),
            pltpu.VMEM((2, 2, steps, half, width), BF16),
            pltpu.VMEM((NZ, 2, tok, depth), BF16),
            pltpu.VMEM((NC, tok, depth), BF16),
            pltpu.VMEM((depth, width), BF16),
            pltpu.VMEM((tok, depth), BF16),
            dma((4,)),
            dma((2, 4, 2)), dma((2, 4, 2)),
            dma((2, 2, steps)), dma((2, 2, steps)),
            dma((NZ, 2)), dma((NZ, 2)),
            dma((NZ,)), dma((NZ,)),
            dma((2, 2, steps)), dma((2, 2, steps)),
            dma((NZ, 2)), dma((NC,)),
            dma((3,)),
        ],
        compiler_params=pltpu.CompilerParams(
            collective_id=0, has_side_effects=True, vmem_limit_bytes=44 * 1024 * 1024
        ),
        cost_estimate=pl.CostEstimate(
            flops=6 * tokens * depth * width, bytes_accessed=4 * depth * width + 4 * tok * (width + depth), transcendentals=0
        ),
    )(*(pltpu.with_memory_space_constraint(a, pltpu.HBM) for a in (inputs, weight, mask, cotangent)))
    shapes = ((tok, width), (tok, depth), (depth, width))
    return pl.pallas_call(
        finish,
        out_shape=tuple(jax.ShapeDtypeStruct(shape, BF16) for shape in shapes),
        in_specs=[pl.BlockSpec(memory_space=pltpu.VMEM)] * 4,
        out_specs=(hbm,) * 3,
        scratch_shapes=[pltpu.VMEM((tok, width), BF16), dma((7,))],
        compiler_params=pltpu.CompilerParams(vmem_limit_bytes=8 * 1024 * 1024),
    )(*results)


def solution(mesh):
    placed = (P("col", "row"), P("row", "col"), P("row", "col"), P("row", "col"))
    return jax.shard_map(
        local,
        mesh=mesh,
        in_specs=placed,
        out_specs=(P("row", "col"), P("col", "row"), P("row", "col")),
        check_vma=False,
    )
```
